128 devices in a mesh: gx: 4 (over x), gy: 32 (over y, z, core).
Axes of the slice: x: 4, y: 4, z: 4, core: 2. Of those that a mesh axis runs over, the one named last changes fastest.
Arguments:
- velocity: float32 [3, 32, 1024, 128], P(None, 'gx', 'gy'), may hold values from -4 to 4
- basis: bfloat16 [64, 3, 32, 1024, 128], P(None, None, 'gx', 'gy'), may hold values from -100 to 100
- snapshots: bfloat16 [63, 3, 32, 1024, 128], P(None, None, 'gx', 'gy'), may hold values from -100 to 100
Outputs:
- advanced: float32 [3, 32, 1024, 128], P(None, 'gx', 'gy')
- factor: float32 [128, 128], replicated
The draws below stay inside these ranges and needn't reach their ends.
All inputs are finite; a program needn't handle non-finite values.
Results may differ from the reference program's by a relative error of at most 0.0003.
Values sent between devices are 32-bit elements; how exact they have to be, the bound alone decides.
No kernel may reach another device: no remote copies, remote signals or barrier semaphores. Data moves between devices by JAX's collectives and lax.ppermute only.
A program may use at most 128 MiB of HBM per device.

```python
import math
import jax
import jax.numpy as jnp
from jax import lax

NY = 128
BASIS = 64
SNAP = 64
NX = 32
NZ = 1024


def flow_field(key):
    flow_keys = jax.random.split(jax.random.fold_in(key, 5), 1)
    full_shape = (3, NX, NZ, NY)
    entries = jnp.clip(jax.random.normal(flow_keys[0], full_shape, jnp.float32), -4.0, 4.0)
    return entries


def scaled_field(key, flow, columns, share_lo, share_hi):
    draw_keys = jax.random.split(key, 5)
    full_shape = (columns, 3, NX, NZ, NY)
    col_scale = jnp.exp(jax.random.uniform(draw_keys[1], (columns, 1, 1, 1, 1), jnp.float32, math.log(0.3), math.log(3.0)))
    row_scale = jnp.exp(jax.random.uniform(draw_keys[2], (1, 1, NX, NZ, 1), jnp.float32, math.log(0.3), math.log(3.0)))
    spanwise_rise = jnp.exp(math.log(3.0) * jnp.arange(NZ, dtype=jnp.float32) / NZ).reshape(1, 1, 1, NZ, 1) / 1.7
    shares = jax.random.uniform(draw_keys[4], (columns, 1, 1, 1, 1), jnp.float32, share_lo, share_hi)
    noise = jnp.clip(jax.random.normal(draw_keys[0], full_shape, jnp.float32), -4.0, 4.0)
    entries = jnp.clip(shares * flow[None] + noise, -6.0, 6.0)
    return (entries * col_scale * row_scale * spanwise_rise).astype(jnp.bfloat16)


def draw_velocity(key, part):
    return flow_field(key)


def draw_basis(key, part):
    return scaled_field(jax.random.fold_in(key, 11), flow_field(key), BASIS, 0.0, 0.6)


def draw_snapshots(key, part):
    return scaled_field(jax.random.fold_in(key, 23), flow_field(key), SNAP - 1, 0.4, 1.0)


def setup_inputs(seed: int = 0) -> dict:
    streams_of = jax.random.split(jax.random.key(seed), 4)
    velocity = draw_velocity(jax.random.fold_in(streams_of[3], 71), 0)
    basis = draw_basis(jax.random.fold_in(streams_of[3], 71), 0)
    snapshots = draw_snapshots(jax.random.fold_in(streams_of[3], 71), 0)
    return dict(velocity=velocity, basis=basis, snapshots=snapshots)


TIME_STEP = 0.0002
VISCOSITY = 0.005
STEP_X = 0.0123
STEP_Z = 0.0092
STRETCH = 2.0

def wall_weights(points):
    positions = jnp.arange(points + 2, dtype=jnp.float32)
    nodes = -jnp.tanh(STRETCH * (1.0 - 2.0 * positions / (points + 1))) / math.tanh(STRETCH)
    below = nodes[1:-1] - nodes[:-2]
    above = nodes[2:] - nodes[1:-1]
    spread = above * below * (above + below)
    return (below * below / spread, -(above * above) / spread, (above * above - below * below) / spread, 2.0 * below / spread, -2.0 * (above + below) / spread, 2.0 * above / spread)

def tendency(widened):
    weights = wall_weights(widened.shape[3])
    center = widened[:, 2:-2, 2:-2, :]
    length_x = center.shape[1]
    length_z = center.shape[2]

    def along_x(offset):
        return widened[:, 2 + offset:2 + offset + length_x, 2:-2, :]

    def along_z(offset):
        return widened[:, 2:-2, 2 + offset:2 + offset + length_z, :]
    slope_x = (-along_x(2) + 8.0 * along_x(1) - 8.0 * along_x(-1) + along_x(-2)) / (12.0 * STEP_X)
    curve_x = (-along_x(2) + 16.0 * along_x(1) - 30.0 * center + 16.0 * along_x(-1) - along_x(-2)) / (12.0 * STEP_X * STEP_X)
    slope_z = (-along_z(2) + 8.0 * along_z(1) - 8.0 * along_z(-1) + along_z(-2)) / (12.0 * STEP_Z)
    curve_z = (-along_z(2) + 16.0 * along_z(1) - 30.0 * center + 16.0 * along_z(-1) - along_z(-2)) / (12.0 * STEP_Z * STEP_Z)
    padded = jnp.pad(center, ((0, 0), (0, 0), (0, 0), (1, 1)))
    upper_vals = padded[..., 2:]
    lower_vals = padded[..., :-2]
    slope_y = weights[0] * upper_vals + weights[1] * lower_vals + weights[2] * center
    curve_y = weights[3] * upper_vals + weights[4] * center + weights[5] * lower_vals
    carried = center[0:1] * slope_x + center[1:2] * slope_y + center[2:3] * slope_z
    return -carried + VISCOSITY * (curve_x + curve_y + curve_z)

def reference(velocity, basis, snapshots):
    margins = ((0, 0), (2, 2), (2, 2), (0, 0))
    widened = jnp.pad(velocity, margins, mode='wrap')
    section_field = velocity + TIME_STEP * tendency(widened)
    widened = jnp.pad(section_field, margins, mode='wrap')
    advanced = 0.5 * (velocity + section_field + TIME_STEP * tendency(widened))
    newest = advanced.astype(jnp.bfloat16)

    def add_slab(index, total):
        basis_slab = lax.dynamic_slice_in_dim(basis, index, 1, 2).reshape(BASIS, -1)
        stored_slab = lax.dynamic_slice_in_dim(snapshots, index, 1, 2).reshape(SNAP - 1, -1)
        newest_slab = lax.dynamic_slice_in_dim(newest, index, 1, 1).reshape(1, -1)
        block = jnp.concatenate([basis_slab, stored_slab, newest_slab], 0)
        return total + jnp.dot(block.astype(jnp.float32), block.T.astype(jnp.float32), preferred_element_type=jnp.float32)
    total = lax.fori_loop(0, NX, add_slab, jnp.zeros((BASIS + SNAP, BASIS + SNAP), jnp.float32))
    gram = total * (1.0 / (3.0 * NX * NZ * NY))
    factor = jnp.linalg.cholesky(gram).T
    return (advanced, factor)
```

```python
import functools
import math

import jax
import jax.numpy as jnp
from jax import lax
from jax.experimental import pallas as pl
from jax.experimental.pallas import tpu as pltpu
from jax.sharding import PartitionSpec as P

TIME_STEP = 0.0002
VISCOSITY = 0.005
STEP_X = 0.0123
STEP_Z = 0.0092
STRETCH = 2.0


def with_halo(cells, sides, width):
    for axis, dim in sides:
        count = lax.axis_size(axis)
        head = lax.slice_in_dim(cells, 0, width, axis=dim)
        tail = lax.slice_in_dim(cells, cells.shape[dim] - width, cells.shape[dim], axis=dim)
        cells = jnp.concatenate(
            [
                lax.ppermute(tail, axis, [(i, (i + 1) % count) for i in range(count)]),
                cells,
                lax.ppermute(head, axis, [((i + 1) % count, i) for i in range(count)]),
            ],
            axis=dim,
        )
    return cells


def wall_weights(points):
    positions = jnp.arange(points + 2, dtype=jnp.float32)
    nodes = -jnp.tanh(STRETCH * (1.0 - 2.0 * positions / (points + 1))) / math.tanh(STRETCH)
    below = nodes[1:-1] - nodes[:-2]
    above = nodes[2:] - nodes[1:-1]
    spread = above * below * (above + below)
    return (
        below * below / spread,
        -(above * above) / spread,
        (above * above - below * below) / spread,
        2.0 * below / spread,
        -2.0 * (above + below) / spread,
        2.0 * above / spread,
    )


def tendency(widened):
    weights = wall_weights(widened.shape[3])
    center = widened[:, 2:-2, 2:-2, :]
    length_x = center.shape[1]
    length_z = center.shape[2]

    def along_x(offset):
        return widened[:, 2 + offset : 2 + offset + length_x, 2:-2, :]

    def along_z(offset):
        return widened[:, 2:-2, 2 + offset : 2 + offset + length_z, :]

    slope_x = (-along_x(2) + 8.0 * along_x(1) - 8.0 * along_x(-1) + along_x(-2)) / (12.0 * STEP_X)
    curve_x = (
        -along_x(2) + 16.0 * along_x(1) - 30.0 * center + 16.0 * along_x(-1) - along_x(-2)
    ) / (12.0 * STEP_X * STEP_X)
    slope_z = (-along_z(2) + 8.0 * along_z(1) - 8.0 * along_z(-1) + along_z(-2)) / (12.0 * STEP_Z)
    curve_z = (
        -along_z(2) + 16.0 * along_z(1) - 30.0 * center + 16.0 * along_z(-1) - along_z(-2)
    ) / (12.0 * STEP_Z * STEP_Z)
    padded = jnp.pad(center, ((0, 0), (0, 0), (0, 0), (1, 1)))
    upper_vals = padded[..., 2:]
    lower_vals = padded[..., :-2]
    slope_y = weights[0] * upper_vals + weights[1] * lower_vals + weights[2] * center
    curve_y = weights[3] * upper_vals + weights[4] * center + weights[5] * lower_vals
    carried = center[0:1] * slope_x + center[1:2] * slope_y + center[2:3] * slope_z
    return -carried + VISCOSITY * (curve_x + curve_y + curve_z)


CHUNKS = (96, 96, 96, 96)
MXU_STEP = 16


def gram_kernel(scale, basis_ref, stored_ref, newest_ref, gram_ref, block, wide, folded, sems):
    n_basis = basis_ref.shape[0]
    n_stored = stored_ref.shape[0]
    starts = [sum(CHUNKS[:q]) for q in range(len(CHUNKS))]

    def issue(q):
        span = pl.ds(starts[q], CHUNKS[q])

        def send(source, column):
            pltpu.make_async_copy(
                source.at[span], block.at[span, pl.ds(pl.multiple_of(2 * column, 2), 2)], sems.at[q]
            ).start()

        @pl.loop(0, n_basis)
        def _(c):
            send(basis_ref.at[c], c)

        @pl.loop(0, n_stored)
        def _(c):
            send(stored_ref.at[c], n_basis + c)

        send(newest_ref, n_basis + n_stored)

    def body(acc0, acc1):
        accs = (acc0, acc1)
        issue(0)
        issue(1)
        for q in range(len(CHUNKS)):
            if q + 2 < len(CHUNKS):
                issue(q + 2)
            span = block.at[pl.ds(starts[q], CHUNKS[q])]
            pltpu.make_async_copy(span, span, sems.at[q]).wait()

            @pl.loop(0, CHUNKS[q] // MXU_STEP)
            def _(t):
                base = starts[q] + t * MXU_STEP
                for u in range(MXU_STEP // 2):
                    unit = u % 2
                    register = (u // 2) % 2
                    rows = jnp.concatenate([block[base + 2 * u], block[base + 2 * u + 1]], axis=1)
                    pltpu.matmul_push_rhs(rows, register, unit, transpose=True)
                    pltpu.matmul_acc_lhs(accs[unit], rows, load_staged_rhs=register)

        total = pltpu.matmul_pop(acc0) + pltpu.matmul_pop(acc1)
        for h in range(2):
            wide[h] = total[:, 128 * h : 128 * (h + 1)]

    pl.run_scoped(
        body, pltpu.ACC(0)((256, 256), jnp.float32), pltpu.ACC(1)((256, 256), jnp.float32)
    )
    lane = lax.broadcasted_iota(jnp.int32, (128, 128), 1)
    for h in range(2):
        even = wide[h, pl.ds(0, 128, stride=2), :]
        odd = wide[h, pl.ds(1, 128, stride=2), :]
        folded[128 * h : 128 * (h + 1)] = (jnp.where(lane % 2 == 0, even, odd) * scale).T
    gram_ref[...] = folded[pl.ds(0, 128, stride=2), :] + folded[pl.ds(1, 128, stride=2), :]


def pair_rows(field, lead):
    return field.reshape(*field.shape[:lead], -1, 2, field.shape[-1])


def local_gram(basis, stored, newest, scale):
    basis = pair_rows(basis, 1)
    stored = pair_rows(stored, 1)
    newest = pair_rows(newest, 0)
    hbm = pl.BlockSpec(memory_space=pltpu.HBM)
    return pl.pallas_call(
        functools.partial(gram_kernel, scale),
        out_shape=jax.ShapeDtypeStruct((128, 128), jnp.float32),
        in_specs=[hbm, hbm, hbm],
        out_specs=pl.BlockSpec(memory_space=pltpu.VMEM),
        scratch_shapes=[
            pltpu.VMEM((basis.shape[1], 256, 128), jnp.bfloat16),
            pltpu.VMEM((2, 256, 128), jnp.float32),
            pltpu.VMEM((256, 128), jnp.float32),
            pltpu.SemaphoreType.DMA((len(CHUNKS),)),
        ],
        compiler_params=pltpu.CompilerParams(vmem_limit_bytes=40 * 2**20),
        name="gram",
    )(basis, stored, newest)


def swap_cores(part, count):
    return lax.ppermute(part, "gy", [(i, i ^ 1) for i in range(count)])


def ring_sum(part, axis, count, stride):
    def target(i, d):
        place = (i // stride) % 4
        return i + ((place + d) % 4 - place) * stride

    moved = [
        lax.ppermute(part, axis, [(i, target(i, d)) for i in range(count)]) for d in (1, 2, 3)
    ]
    return (part + moved[1]) + (moved[0] + moved[2])


def total_gram(gram):
    count = lax.axis_size("gy")
    half = gram.shape[0] // 2
    core = lax.axis_index("gy") % 2
    mine = lax.dynamic_slice_in_dim(gram, core * half, half, 0)
    other = lax.dynamic_slice_in_dim(gram, (1 - core) * half, half, 0)
    part = mine + swap_cores(other, count)
    part = ring_sum(part, "gy", count, 2)
    part = ring_sum(part, "gy", count, 8)
    part = ring_sum(part, "gx", 4, 1)
    rest = swap_cores(part, count)
    low = jnp.where(core == 0, part, rest)
    high = jnp.where(core == 0, rest, part)
    return jnp.concatenate([low, high], 0)


def widen_once(field):
    return with_halo(field, (("gx", 1), ("gy", 2)), 2)


def local(velocity, basis, snapshots):
    section_field = velocity + TIME_STEP * tendency(widen_once(velocity))
    advanced = 0.5 * (velocity + section_field + TIME_STEP * tendency(widen_once(section_field)))
    newest = advanced.astype(jnp.bfloat16)
    total_rows = (
        3.0
        * velocity.shape[1]
        * lax.axis_size("gx")
        * velocity.shape[2]
        * lax.axis_size("gy")
        * velocity.shape[3]
    )
    gram = local_gram(basis, snapshots, newest, 1.0 / total_rows)
    factor = jnp.linalg.cholesky(total_gram(gram)).T
    return (advanced, factor)


def solution(mesh):
    return jax.shard_map(
        local,
        mesh=mesh,
        in_specs=(
            P(None, "gx", "gy", None),
            P(None, None, "gx", "gy", None),
            P(None, None, "gx", "gy", None),
        ),
        out_specs=(P(None, "gx", "gy", None), P()),
        check_vma=False,
    )
```

```python
import functools
import math

import jax
import jax.numpy as jnp
from jax import lax
from jax.experimental import pallas as pl
from jax.experimental.pallas import tpu as pltpu
from jax.sharding import PartitionSpec as P

TIME_STEP = 0.0002
VISCOSITY = 0.005
STEP_X = 0.0123
STEP_Z = 0.0092
STRETCH = 2.0


def wall_weights(points):
    positions = jnp.arange(points + 2, dtype=jnp.float32)
    nodes = -jnp.tanh(STRETCH * (1.0 - 2.0 * positions / (points + 1))) / math.tanh(STRETCH)
    below = nodes[1:-1] - nodes[:-2]
    above = nodes[2:] - nodes[1:-1]
    spread = above * below * (above + below)
    return (
        below * below / spread,
        -(above * above) / spread,
        (above * above - below * below) / spread,
        2.0 * below / spread,
        -2.0 * (above + below) / spread,
        2.0 * above / spread,
    )


def tendency(field, place, first, count, weights):
    def rows(c, dx, dz):
        return field[c, place + dx, pl.ds(first + dz, count), :]

    centers = [rows(c, 0, 0) for c in range(3)]
    lanes = centers[0].shape[1]
    along_x = centers[0] * (1.0 / (12.0 * STEP_X))
    along_z = centers[2] * (1.0 / (12.0 * STEP_Z))
    results = []
    for c in range(3):
        center = centers[c]
        x2, x1, x_1, x_2 = (rows(c, d, 0) for d in (2, 1, -1, -2))
        z2, z1, z_1, z_2 = (rows(c, 0, d) for d in (2, 1, -1, -2))
        upper = pltpu.roll(center, lanes - 1, 1)
        lower = pltpu.roll(center, 1, 1)
        slope_x = 8.0 * (x1 - x_1) - (x2 - x_2)
        slope_z = 8.0 * (z1 - z_1) - (z2 - z_2)
        slope_y = weights[0] * upper + weights[1] * lower + weights[2] * center
        curve_x = 16.0 * (x1 + x_1) - (x2 + x_2) - 30.0 * center
        curve_z = 16.0 * (z1 + z_1) - (z2 + z_2) - 30.0 * center
        curve_y = weights[3] * upper + weights[4] * center + weights[5] * lower
        carried = along_x * slope_x + centers[1] * slope_y + along_z * slope_z
        spread = (
            curve_x * (VISCOSITY / (12.0 * STEP_X * STEP_X))
            + curve_z * (VISCOSITY / (12.0 * STEP_Z * STEP_Z))
            + curve_y
        )
        results.append((center, spread - carried))
    return results


CHUNKS = (160, 128, 96)
MXU_STEP = 32


def step_kernel(
    scale,
    velocity_ref,
    left_ref,
    right_ref,
    behind_ref,
    ahead_ref,
    weights_ref,
    basis_ref,
    stored_ref,
    advanced_ref,
    gram_ref,
    block,
    wide,
    folded,
    field,
    section,
    advanced,
    sems,
    halo_sems,
    out_sem,
):
    n_basis = basis_ref.shape[0]
    n_stored = stored_ref.shape[0]
    length_x, length_z = velocity_ref.shape[1:3]
    starts = [sum(CHUNKS[:q]) for q in range(len(CHUNKS))]

    halos = [
        pltpu.make_async_copy(source, target, halo_sems.at[i])
        for i, (source, target) in enumerate(
            (
                (velocity_ref, field.at[:, pl.ds(4, length_x), pl.ds(4, length_z)]),
                (left_ref, field.at[:, pl.ds(0, 4), pl.ds(4, length_z)]),
                (right_ref, field.at[:, pl.ds(4 + length_x, 4), pl.ds(4, length_z)]),
                (behind_ref, field.at[:, pl.ds(2, 4 + length_x), pl.ds(0, 4)]),
                (ahead_ref, field.at[:, pl.ds(2, 4 + length_x), pl.ds(4 + length_z, 4)]),
            )
        )
    ]
    for halo in halos:
        halo.start()

    def issue(q):
        span = pl.ds(starts[q], CHUNKS[q])

        def send(source, column):
            pltpu.make_async_copy(
                source.at[span], block.at[span, pl.ds(pl.multiple_of(2 * column, 2), 2)], sems.at[q]
            ).start()

        def from_basis(c, carry):
            send(basis_ref.at[c], c)
            return carry

        def from_stored(c, carry):
            send(stored_ref.at[c], n_basis + c)
            return carry

        lax.fori_loop(0, n_basis, from_basis, 0, unroll=8)
        lax.fori_loop(0, n_stored, from_stored, 0, unroll=9)

    for q in range(len(CHUNKS)):
        issue(q)
    for halo in halos:
        halo.wait()

    weights = [weights_ref[i : i + 1, :] for i in range(6)]

    @pl.loop(0, length_x + 4)
    def _(x):
        for c, (center, change) in enumerate(tendency(field, x + 2, 2, length_z + 8, weights)):
            section[c, x, pl.ds(0, length_z + 8), :] = center + TIME_STEP * change

    last = 2 * (n_basis + n_stored)

    @pl.loop(0, length_x)
    def _(x):
        for c, (center, change) in enumerate(tendency(section, x + 2, 2, length_z, weights)):
            begin = field[c, x + 4, pl.ds(4, length_z), :]
            end = 0.5 * (begin + center + TIME_STEP * change)
            advanced[c, x] = end
            rounded = end.astype(jnp.bfloat16)
            pair = (c * length_x + x) * (length_z // 2)
            for j in range(length_z // 2):
                block[pair + j, last : last + 2, :] = rounded[2 * j : 2 * j + 2, :]

    leave = pltpu.make_async_copy(advanced, advanced_ref, out_sem.at[0])
    leave.start()

    def body(acc0, acc1):
        accs = (acc0, acc1)
        for q in range(len(CHUNKS)):
            arrived = block.at[pl.ds(starts[q], CHUNKS[q]), pl.ds(0, last)]
            pltpu.make_async_copy(arrived, arrived, sems.at[q]).wait()

            @pl.loop(0, CHUNKS[q] // MXU_STEP)
            def _(t):
                base = starts[q] + t * MXU_STEP
                for u in range(MXU_STEP // 2):
                    unit = u % 2
                    register = (u // 2) % 2
                    rows = jnp.concatenate([block[base + 2 * u], block[base + 2 * u + 1]], axis=1)
                    pltpu.matmul_push_rhs(rows, register, unit, transpose=True)
                    pltpu.matmul_acc_lhs(accs[unit], rows, load_staged_rhs=register)

        total = pltpu.matmul_pop(acc0) + pltpu.matmul_pop(acc1)
        for h in range(2):
            wide[h] = total[:, 128 * h : 128 * (h + 1)]

    pl.run_scoped(
        body, pltpu.ACC(0)((256, 256), jnp.float32), pltpu.ACC(1)((256, 256), jnp.float32)
    )
    lane = lax.broadcasted_iota(jnp.int32, (128, 128), 1)
    for h in range(2):
        even = wide[h, pl.ds(0, 128, stride=2), :]
        odd = wide[h, pl.ds(1, 128, stride=2), :]
        folded[128 * h : 128 * (h + 1)] = (jnp.where(lane % 2 == 0, even, odd) * scale).T
    gram_ref[...] = folded[pl.ds(0, 128, stride=2), :] + folded[pl.ds(1, 128, stride=2), :]
    leave.wait()


def pair_rows(fields):
    return fields.reshape(fields.shape[0], -1, 2, fields.shape[-1])


def step_and_gram(velocity, halos, weights, basis, stored, scale):
    basis = pair_rows(basis)
    stored = pair_rows(stored)
    length_x, length_z, lanes = velocity.shape[1:]
    hbm = pl.BlockSpec(memory_space=pltpu.HBM)
    free = pl.BlockSpec(memory_space=pl.ANY)
    vmem = pl.BlockSpec(memory_space=pltpu.VMEM)
    return pl.pallas_call(
        functools.partial(step_kernel, scale),
        out_shape=(
            jax.ShapeDtypeStruct(velocity.shape, jnp.float32),
            jax.ShapeDtypeStruct((128, 128), jnp.float32),
        ),
        in_specs=[free, free, free, free, free, vmem, hbm, hbm],
        out_specs=(hbm, vmem),
        scratch_shapes=[
            pltpu.VMEM((basis.shape[1], 256, lanes), jnp.bfloat16),
            pltpu.VMEM((2, 256, 128), jnp.float32),
            pltpu.VMEM((256, 128), jnp.float32),
            pltpu.VMEM((3, length_x + 8, length_z + 16, lanes), jnp.float32),
            pltpu.VMEM((3, length_x + 4, length_z + 8, lanes), jnp.float32),
            pltpu.VMEM(velocity.shape, jnp.float32),
            pltpu.SemaphoreType.DMA((len(CHUNKS),)),
            pltpu.SemaphoreType.DMA((5,)),
            pltpu.SemaphoreType.DMA((1,)),
        ],
        compiler_params=pltpu.CompilerParams(vmem_limit_bytes=60 * 2**20),
        name="step_gram",
    )(velocity, *halos, weights, basis, stored)


def shift(part, axis, step):
    count = lax.axis_size(axis)
    return lax.ppermute(part, axis, [(i, (i + step) % count) for i in range(count)])


def exchange(velocity):
    left = shift(velocity[:, -4:], "gx", 1)
    right = shift(velocity[:, :4], "gx", -1)
    wide = jnp.concatenate([left[:, 2:], velocity, right[:, :2]], axis=1)
    behind = shift(wide[:, :, -4:], "gy", 1)
    ahead = shift(wide[:, :, :4], "gy", -1)
    return left, right, behind, ahead


def wall_rows(points):
    up, down, here, curve_down, curve_here, curve_up = wall_weights(points)
    lane = jnp.arange(points)
    has_up = lane < points - 1
    has_down = lane > 0
    return jnp.stack(
        [
            jnp.where(has_up, up, 0.0),
            jnp.where(has_down, down, 0.0),
            here,
            VISCOSITY * jnp.where(has_up, curve_down, 0.0),
            VISCOSITY * curve_here,
            VISCOSITY * jnp.where(has_down, curve_up, 0.0),
            jnp.zeros_like(here),
            jnp.zeros_like(here),
        ]
    )


def swap_cores(part, count):
    return lax.ppermute(part, "gy", [(i, i ^ 1) for i in range(count)])


def ring_sum(part, axis, count, stride):
    def target(i, d):
        place = (i // stride) % 4
        return i + ((place + d) % 4 - place) * stride

    moved = [
        lax.ppermute(part, axis, [(i, target(i, d)) for i in range(count)]) for d in (1, 2, 3)
    ]
    return (part + moved[1]) + (moved[0] + moved[2])


def total_gram(gram):
    count = lax.axis_size("gy")
    half = gram.shape[0] // 2
    core = lax.axis_index("gy") % 2
    mine = lax.dynamic_slice_in_dim(gram, core * half, half, 0)
    other = lax.dynamic_slice_in_dim(gram, (1 - core) * half, half, 0)
    part = mine + swap_cores(other, count)
    part = ring_sum(part, "gy", count, 2)
    part = ring_sum(part, "gy", count, 8)
    part = ring_sum(part, "gx", 4, 1)
    rest = swap_cores(part, count)
    low = jnp.where(core == 0, part, rest)
    high = jnp.where(core == 0, rest, part)
    return jnp.concatenate([low, high], 0)


def local(velocity, basis, snapshots):
    total_rows = (
        3.0
        * velocity.shape[1]
        * lax.axis_size("gx")
        * velocity.shape[2]
        * lax.axis_size("gy")
        * velocity.shape[3]
    )
    halos = exchange(velocity)
    weights = wall_rows(velocity.shape[3])
    advanced, gram = step_and_gram(velocity, halos, weights, basis, snapshots, 1.0 / total_rows)
    factor = jnp.linalg.cholesky(total_gram(gram)).T
    return (advanced, factor)


def solution(mesh):
    return jax.shard_map(
        local,
        mesh=mesh,
        in_specs=(
            P(None, "gx", "gy", None),
            P(None, None, "gx", "gy", None),
            P(None, None, "gx", "gy", None),
        ),
        out_specs=(P(None, "gx", "gy", None), P()),
        check_vma=False,
    )
```

```python
import functools
import math

import jax
import jax.numpy as jnp
from jax import lax
from jax.experimental import pallas as pl
from jax.experimental.pallas import tpu as pltpu
from jax.sharding import PartitionSpec as P

TIME_STEP = 0.0002
VISCOSITY = 0.005
STEP_X = 0.0123
STEP_Z = 0.0092
STRETCH = 2.0


def wall_weights(points):
    positions = jnp.arange(points + 2, dtype=jnp.float32)
    nodes = -jnp.tanh(STRETCH * (1.0 - 2.0 * positions / (points + 1))) / math.tanh(STRETCH)
    below = nodes[1:-1] - nodes[:-2]
    above = nodes[2:] - nodes[1:-1]
    spread = above * below * (above + below)
    return (
        below * below / spread,
        -(above * above) / spread,
        (above * above - below * below) / spread,
        2.0 * below / spread,
        -2.0 * (above + below) / spread,
        2.0 * above / spread,
    )


def tendency(field, place, first, count, weights):
    def rows(c, dx, dz):
        return field[c, place + dx, pl.ds(first + dz, count), :]

    centers = [rows(c, 0, 0) for c in range(3)]
    lanes = centers[0].shape[1]
    along_x = centers[0] * (1.0 / (12.0 * STEP_X))
    along_z = centers[2] * (1.0 / (12.0 * STEP_Z))
    results = []
    for c in range(3):
        center = centers[c]
        x2, x1, x_1, x_2 = (rows(c, d, 0) for d in (2, 1, -1, -2))
        z2, z1, z_1, z_2 = (rows(c, 0, d) for d in (2, 1, -1, -2))
        upper = pltpu.roll(center, lanes - 1, 1)
        lower = pltpu.roll(center, 1, 1)
        slope_x = 8.0 * (x1 - x_1) - (x2 - x_2)
        slope_z = 8.0 * (z1 - z_1) - (z2 - z_2)
        slope_y = weights[0] * upper + weights[1] * lower + weights[2] * center
        curve_x = 16.0 * (x1 + x_1) - (x2 + x_2) - 30.0 * center
        curve_z = 16.0 * (z1 + z_1) - (z2 + z_2) - 30.0 * center
        curve_y = weights[3] * upper + weights[4] * center + weights[5] * lower
        carried = along_x * slope_x + centers[1] * slope_y + along_z * slope_z
        spread = (
            curve_x * (VISCOSITY / (12.0 * STEP_X * STEP_X))
            + curve_z * (VISCOSITY / (12.0 * STEP_Z * STEP_Z))
            + curve_y
        )
        results.append((center, spread - carried))
    return results


CHUNKS = (160, 128, 96)
MXU_STEP = 32


def step_kernel(
    scale,
    velocity_ref,
    left_ref,
    right_ref,
    behind_ref,
    ahead_ref,
    weights_ref,
    basis_ref,
    stored_ref,
    advanced_ref,
    gram_ref,
    block,
    wide,
    folded,
    field,
    section,
    advanced,
    sems,
    halo_sems,
    out_sem,
):
    n_basis = basis_ref.shape[0]
    n_stored = stored_ref.shape[0]
    length_x, length_z = velocity_ref.shape[1:3]
    starts = [sum(CHUNKS[:q]) for q in range(len(CHUNKS))]

    halos = [
        pltpu.make_async_copy(source, target, halo_sems.at[i])
        for i, (source, target) in enumerate(
            (
                (velocity_ref, field.at[:, pl.ds(4, length_x), pl.ds(4, length_z)]),
                (left_ref, field.at[:, pl.ds(0, 4), pl.ds(4, length_z)]),
                (right_ref, field.at[:, pl.ds(4 + length_x, 4), pl.ds(4, length_z)]),
                (behind_ref, field.at[:, pl.ds(2, 4 + length_x), pl.ds(0, 4)]),
                (ahead_ref, field.at[:, pl.ds(2, 4 + length_x), pl.ds(4 + length_z, 4)]),
            )
        )
    ]
    for halo in halos:
        halo.start()

    def issue(q):
        span = pl.ds(starts[q], CHUNKS[q])

        def send(source, column):
            pltpu.make_async_copy(
                source.at[span], block.at[span, pl.ds(pl.multiple_of(2 * column, 2), 2)], sems.at[q]
            ).start()

        def from_basis(c, carry):
            send(basis_ref.at[c], c)
            return carry

        def from_stored(c, carry):
            send(stored_ref.at[c], n_basis + c)
            return carry

        lax.fori_loop(0, n_basis, from_basis, 0, unroll=8)
        lax.fori_loop(0, n_stored, from_stored, 0, unroll=9)

    for q in range(len(CHUNKS)):
        issue(q)
    for halo in halos:
        halo.wait()

    weights = [weights_ref[i : i + 1, :] for i in range(6)]

    @pl.loop(0, length_x + 4)
    def _(x):
        for c, (center, change) in enumerate(tendency(field, x + 2, 2, length_z + 8, weights)):
            section[c, x, pl.ds(0, length_z + 8), :] = center + TIME_STEP * change

    last = 2 * (n_basis + n_stored)

    @pl.loop(0, length_x)
    def _(x):
        for c, (center, change) in enumerate(tendency(section, x + 2, 2, length_z, weights)):
            begin = field[c, x + 4, pl.ds(4, length_z), :]
            end = 0.5 * (begin + center + TIME_STEP * change)
            advanced[c, x] = end
            rounded = end.astype(jnp.bfloat16)
            pair = (c * length_x + x) * (length_z // 2)
            for j in range(length_z // 2):
                block[pair + j, last : last + 2, :] = rounded[2 * j : 2 * j + 2, :]

    leave = pltpu.make_async_copy(advanced, advanced_ref, out_sem.at[0])
    leave.start()

    def body(acc0, acc1):
        accs = (acc0, acc1)
        for q in range(len(CHUNKS)):
            arrived = block.at[pl.ds(starts[q], CHUNKS[q]), pl.ds(0, last)]
            pltpu.make_async_copy(arrived, arrived, sems.at[q]).wait()

            @pl.loop(0, CHUNKS[q] // MXU_STEP)
            def _(t):
                base = starts[q] + t * MXU_STEP
                for u in range(MXU_STEP // 2):
                    unit = u % 2
                    register = (u // 2) % 2
                    rows = jnp.concatenate([block[base + 2 * u], block[base + 2 * u + 1]], axis=1)
                    pltpu.matmul_push_rhs(rows, register, unit, transpose=True)
                    pltpu.matmul_acc_lhs(accs[unit], rows, load_staged_rhs=register)

        total = pltpu.matmul_pop(acc0) + pltpu.matmul_pop(acc1)
        for h in range(2):
            wide[h] = total[:, 128 * h : 128 * (h + 1)]

    pl.run_scoped(
        body, pltpu.ACC(0)((256, 256), jnp.float32), pltpu.ACC(1)((256, 256), jnp.float32)
    )
    lane = lax.broadcasted_iota(jnp.int32, (128, 128), 1)
    for h in range(2):
        even = wide[h, pl.ds(0, 128, stride=2), :]
        odd = wide[h, pl.ds(1, 128, stride=2), :]
        folded[128 * h : 128 * (h + 1)] = (jnp.where(lane % 2 == 0, even, odd) * scale).T
    gram_ref[...] = folded[pl.ds(0, 128, stride=2), :] + folded[pl.ds(1, 128, stride=2), :]
    leave.wait()


def pair_rows(fields):
    return fields.reshape(fields.shape[0], -1, 2, fields.shape[-1])


def step_and_gram(velocity, halos, weights, basis, stored, scale):
    basis = pltpu.with_memory_space_constraint(pair_rows(basis), pltpu.HBM)
    stored = pltpu.with_memory_space_constraint(pair_rows(stored), pltpu.HBM)
    length_x, length_z, lanes = velocity.shape[1:]
    hbm = pl.BlockSpec(memory_space=pltpu.HBM)
    free = pl.BlockSpec(memory_space=pl.ANY)
    vmem = pl.BlockSpec(memory_space=pltpu.VMEM)
    return pl.pallas_call(
        functools.partial(step_kernel, scale),
        out_shape=(
            jax.ShapeDtypeStruct(velocity.shape, jnp.float32),
            jax.ShapeDtypeStruct((128, 128), jnp.float32),
        ),
        in_specs=[free, free, free, free, free, vmem, hbm, hbm],
        out_specs=(hbm, vmem),
        scratch_shapes=[
            pltpu.VMEM((basis.shape[1], 256, lanes), jnp.bfloat16),
            pltpu.VMEM((2, 256, 128), jnp.float32),
            pltpu.VMEM((256, 128), jnp.float32),
            pltpu.VMEM((3, length_x + 8, length_z + 16, lanes), jnp.float32),
            pltpu.VMEM((3, length_x + 4, length_z + 8, lanes), jnp.float32),
            pltpu.VMEM(velocity.shape, jnp.float32),
            pltpu.SemaphoreType.DMA((len(CHUNKS),)),
            pltpu.SemaphoreType.DMA((5,)),
            pltpu.SemaphoreType.DMA((1,)),
        ],
        compiler_params=pltpu.CompilerParams(vmem_limit_bytes=36 * 2**20),
        name="step_gram",
    )(velocity, *halos, weights, basis, stored)


def shift(part, axis, step):
    count = lax.axis_size(axis)
    return lax.ppermute(part, axis, [(i, (i + step) % count) for i in range(count)])


def exchange(velocity):
    tail, head, back, front = lax.optimization_barrier(
        (velocity[:, -4:], velocity[:, :4], velocity[:, :, -4:], velocity[:, :, :4])
    )
    left = shift(tail, "gx", 1)
    right = shift(head, "gx", -1)
    back = jnp.concatenate([left[:, 2:, -4:], back, right[:, :2, -4:]], axis=1)
    front = jnp.concatenate([left[:, 2:, :4], front, right[:, :2, :4]], axis=1)
    behind = shift(back, "gy", 1)
    ahead = shift(front, "gy", -1)
    return left, right, behind, ahead


def wall_rows(points):
    up, down, here, curve_down, curve_here, curve_up = wall_weights(points)
    lane = jnp.arange(points)
    has_up = lane < points - 1
    has_down = lane > 0
    return jnp.stack(
        [
            jnp.where(has_up, up, 0.0),
            jnp.where(has_down, down, 0.0),
            here,
            VISCOSITY * jnp.where(has_up, curve_down, 0.0),
            VISCOSITY * curve_here,
            VISCOSITY * jnp.where(has_down, curve_up, 0.0),
            jnp.zeros_like(here),
            jnp.zeros_like(here),
        ]
    )


def ring_sum(part, size, stride):
    def target(i, d):
        place = (i // stride) % 4
        return i + ((place + d) % 4 - place) * stride

    moved = [
        lax.ppermute(part, ("gx", "gy"), [(i, target(i, d)) for i in range(1, size, 2)])
        for d in (1, 2, 3)
    ]
    return (part + moved[1]) + (moved[0] + moved[2])


def total_gram(gram):
    count = lax.axis_size("gy")
    size = count * lax.axis_size("gx")
    part = gram + lax.ppermute(gram, "gy", [(i, i + 1) for i in range(0, count, 2)])
    for stride in (2, 8, count):
        part = ring_sum(part, size, stride)
    rest = lax.ppermute(part, "gy", [(i + 1, i) for i in range(0, count, 2)])
    return jnp.where(lax.axis_index("gy") % 2 == 1, part, rest)


PANEL = 16


def factor_kernel(gram_ref, factor_ref, work):
    size = gram_ref.shape[0]
    work[...] = gram_ref[...]
    row = lax.broadcasted_iota(jnp.int32, (PANEL, size), 0)
    lane = lax.broadcasted_iota(jnp.int32, (PANEL, size), 1)
    for begin in range(0, size, PANEL):
        end = begin + PANEL
        rows = work[begin:end, :]
        columns = [
            jnp.broadcast_to(rows[:, begin + k : begin + k + 1], (PANEL, size))
            for k in range(PANEL)
        ]
        scales = jnp.zeros((PANEL, size), jnp.float32)
        for j in range(PANEL):
            scale = lax.rsqrt(columns[j][j : j + 1, :])
            below = jnp.where(row > j, columns[j] * scale, 0.0)
            for k in range(j + 1, PANEL):
                columns[k] = columns[k] - below * (columns[k][j : j + 1, :] * scale)
            rows = rows - below * (rows[j : j + 1, :] * scale)
            scales = jnp.where(row == j, jnp.broadcast_to(scale, (PANEL, size)), scales)
        done = jnp.where(lane >= row + begin, rows * scales, 0.0)
        factor_ref[begin:end, :] = done
        if end < size:
            high = done.astype(jnp.bfloat16)
            left = done - high.astype(jnp.float32)
            mid = left.astype(jnp.bfloat16)
            low = (left - mid.astype(jnp.float32)).astype(jnp.bfloat16)
            product = lax.dot_general(
                jnp.concatenate([high, high, mid, high, low, mid], 0),
                jnp.concatenate([high, mid, high, low, high, mid], 0),
                (((0,), (0,)), ((), ())),
                preferred_element_type=jnp.float32,
            )
            work[end:, :] = work[end:, :] - product[end:, :]


def upper_factor(gram):
    return pl.pallas_call(
        factor_kernel,
        out_shape=jax.ShapeDtypeStruct(gram.shape, jnp.float32),
        in_specs=[pl.BlockSpec(memory_space=pltpu.VMEM)],
        out_specs=pl.BlockSpec(memory_space=pltpu.VMEM),
        scratch_shapes=[pltpu.VMEM(gram.shape, jnp.float32)],
        compiler_params=pltpu.CompilerParams(vmem_limit_bytes=8 * 2**20),
        name="upper_factor",
    )(gram)


def local(velocity, basis, snapshots):
    total_rows = (
        3.0
        * velocity.shape[1]
        * lax.axis_size("gx")
        * velocity.shape[2]
        * lax.axis_size("gy")
        * velocity.shape[3]
    )
    halos = exchange(velocity)
    weights = wall_rows(velocity.shape[3])
    advanced, gram = step_and_gram(velocity, halos, weights, basis, snapshots, 1.0 / total_rows)
    factor = upper_factor(total_gram(gram))
    return (advanced, factor)


def solution(mesh):
    return jax.shard_map(
        local,
        mesh=mesh,
        in_specs=(
            P(None, "gx", "gy", None),
            P(None, None, "gx", "gy", None),
            P(None, None, "gx", "gy", None),
        ),
        out_specs=(P(None, "gx", "gy", None), P()),
        check_vma=False,
    )
```

```python
import functools
import math

import jax
import jax.numpy as jnp
from jax import lax
from jax.experimental import pallas as pl
from jax.experimental.pallas import tpu as pltpu
from jax.sharding import PartitionSpec as P

TIME_STEP = 0.0002
VISCOSITY = 0.005
STEP_X = 0.0123
STEP_Z = 0.0092
STRETCH = 2.0


def wall_weights(points):
    positions = jnp.arange(points + 2, dtype=jnp.float32)
    nodes = -jnp.tanh(STRETCH * (1.0 - 2.0 * positions / (points + 1))) / math.tanh(STRETCH)
    below = nodes[1:-1] - nodes[:-2]
    above = nodes[2:] - nodes[1:-1]
    spread = above * below * (above + below)
    return (
        below * below / spread,
        -(above * above) / spread,
        (above * above - below * below) / spread,
        2.0 * below / spread,
        -2.0 * (above + below) / spread,
        2.0 * above / spread,
    )


def tendency(field, place, first, count, weights):
    def rows(c, dx, dz):
        return field[c, place + dx, pl.ds(first + dz, count), :]

    centers = [rows(c, 0, 0) for c in range(3)]
    lanes = centers[0].shape[1]
    along_x = centers[0] * (1.0 / (12.0 * STEP_X))
    along_z = centers[2] * (1.0 / (12.0 * STEP_Z))
    results = []
    for c in range(3):
        center = centers[c]
        x2, x1, x_1, x_2 = (rows(c, d, 0) for d in (2, 1, -1, -2))
        z2, z1, z_1, z_2 = (rows(c, 0, d) for d in (2, 1, -1, -2))
        upper = pltpu.roll(center, lanes - 1, 1)
        lower = pltpu.roll(center, 1, 1)
        slope_x = 8.0 * (x1 - x_1) - (x2 - x_2)
        slope_z = 8.0 * (z1 - z_1) - (z2 - z_2)
        slope_y = weights[0] * upper + weights[1] * lower + weights[2] * center
        curve_x = 16.0 * (x1 + x_1) - (x2 + x_2) - 30.0 * center
        curve_z = 16.0 * (z1 + z_1) - (z2 + z_2) - 30.0 * center
        curve_y = weights[3] * upper + weights[4] * center + weights[5] * lower
        carried = along_x * slope_x + centers[1] * slope_y + along_z * slope_z
        spread = (
            curve_x * (VISCOSITY / (12.0 * STEP_X * STEP_X))
            + curve_z * (VISCOSITY / (12.0 * STEP_Z * STEP_Z))
            + curve_y
        )
        results.append((center, spread - carried))
    return results


CHUNKS = (160, 128, 96)
MXU_STEP = 32


def step_kernel(
    scale,
    velocity_ref,
    left_ref,
    right_ref,
    behind_ref,
    ahead_ref,
    weights_ref,
    basis_ref,
    stored_ref,
    advanced_ref,
    gram_ref,
    block,
    wide,
    folded,
    field,
    section,
    advanced,
    sems,
    halo_sems,
    out_sem,
):
    n_basis = basis_ref.shape[0]
    n_stored = stored_ref.shape[0]
    length_x, length_z = velocity_ref.shape[1:3]
    starts = [sum(CHUNKS[:q]) for q in range(len(CHUNKS))]

    halos = [
        pltpu.make_async_copy(source, target, halo_sems.at[i])
        for i, (source, target) in enumerate(
            (
                (velocity_ref, field.at[:, pl.ds(4, length_x), pl.ds(4, length_z)]),
                (left_ref, field.at[:, pl.ds(0, 4), pl.ds(4, length_z)]),
                (right_ref, field.at[:, pl.ds(4 + length_x, 4), pl.ds(4, length_z)]),
                (behind_ref, field.at[:, pl.ds(2, 4 + length_x), pl.ds(0, 4)]),
                (ahead_ref, field.at[:, pl.ds(2, 4 + length_x), pl.ds(4 + length_z, 4)]),
            )
        )
    ]
    for halo in halos:
        halo.start()

    def issue(q):
        span = pl.ds(starts[q], CHUNKS[q])

        def send(source, column):
            pltpu.make_async_copy(
                source.at[span], block.at[span, pl.ds(pl.multiple_of(2 * column, 2), 2)], sems.at[q]
            ).start()

        def from_basis(c, carry):
            send(basis_ref.at[c], c)
            return carry

        def from_stored(c, carry):
            send(stored_ref.at[c], n_basis + c)
            return carry

        lax.fori_loop(0, n_basis, from_basis, 0, unroll=8)
        lax.fori_loop(0, n_stored, from_stored, 0, unroll=9)

    for q in range(len(CHUNKS)):
        issue(q)
    for halo in halos:
        halo.wait()

    weights = [weights_ref[i : i + 1, :] for i in range(6)]

    @pl.loop(0, length_x + 4)
    def _(x):
        for c, (center, change) in enumerate(tendency(field, x + 2, 2, length_z + 8, weights)):
            section[c, x, pl.ds(0, length_z + 8), :] = center + TIME_STEP * change

    last = 2 * (n_basis + n_stored)

    @pl.loop(0, length_x)
    def _(x):
        for c, (center, change) in enumerate(tendency(section, x + 2, 2, length_z, weights)):
            begin = field[c, x + 4, pl.ds(4, length_z), :]
            end = 0.5 * (begin + center + TIME_STEP * change)
            advanced[c, x] = end
            rounded = end.astype(jnp.bfloat16)
            pair = (c * length_x + x) * (length_z // 2)
            for j in range(length_z // 2):
                block[pair + j, last : last + 2, :] = rounded[2 * j : 2 * j + 2, :]

    leave = pltpu.make_async_copy(advanced, advanced_ref, out_sem.at[0])
    leave.start()

    def body(acc0, acc1):
        accs = (acc0, acc1)
        for q in range(len(CHUNKS)):
            arrived = block.at[pl.ds(starts[q], CHUNKS[q]), pl.ds(0, last)]
            pltpu.make_async_copy(arrived, arrived, sems.at[q]).wait()

            @pl.loop(0, CHUNKS[q] // MXU_STEP)
            def _(t):
                base = starts[q] + t * MXU_STEP
                for u in range(MXU_STEP // 2):
                    unit = u % 2
                    register = (u // 2) % 2
                    rows = jnp.concatenate([block[base + 2 * u], block[base + 2 * u + 1]], axis=1)
                    pltpu.matmul_push_rhs(rows, register, unit, transpose=True)
                    pltpu.matmul_acc_lhs(accs[unit], rows, load_staged_rhs=register)

        total = pltpu.matmul_pop(acc0) + pltpu.matmul_pop(acc1)
        for h in range(2):
            wide[h] = total[:, 128 * h : 128 * (h + 1)]

    pl.run_scoped(
        body, pltpu.ACC(0)((256, 256), jnp.float32), pltpu.ACC(1)((256, 256), jnp.float32)
    )
    lane = lax.broadcasted_iota(jnp.int32, (128, 128), 1)
    for h in range(2):
        even = wide[h, pl.ds(0, 128, stride=2), :]
        odd = wide[h, pl.ds(1, 128, stride=2), :]
        folded[128 * h : 128 * (h + 1)] = (jnp.where(lane % 2 == 0, even, odd) * scale).T
    gram_ref[...] = folded[pl.ds(0, 128, stride=2), :] + folded[pl.ds(1, 128, stride=2), :]
    leave.wait()


def pair_rows(fields):
    return fields.reshape(fields.shape[0], -1, 2, fields.shape[-1])


def step_and_gram(velocity, halos, weights, basis, stored, scale):
    basis = pltpu.with_memory_space_constraint(pair_rows(basis), pltpu.HBM)
    stored = pltpu.with_memory_space_constraint(pair_rows(stored), pltpu.HBM)
    velocity = pltpu.with_memory_space_constraint(velocity, pltpu.HBM)
    length_x, length_z, lanes = velocity.shape[1:]
    hbm = pl.BlockSpec(memory_space=pltpu.HBM)
    free = pl.BlockSpec(memory_space=pl.ANY)
    vmem = pl.BlockSpec(memory_space=pltpu.VMEM)
    return pl.pallas_call(
        functools.partial(step_kernel, scale),
        out_shape=(
            jax.ShapeDtypeStruct(velocity.shape, jnp.float32),
            jax.ShapeDtypeStruct((128, 128), jnp.float32),
        ),
        in_specs=[hbm, free, free, free, free, vmem, hbm, hbm],
        out_specs=(hbm, vmem),
        scratch_shapes=[
            pltpu.VMEM((basis.shape[1], 256, lanes), jnp.bfloat16),
            pltpu.VMEM((2, 256, 128), jnp.float32),
            pltpu.VMEM((256, 128), jnp.float32),
            pltpu.VMEM((3, length_x + 8, length_z + 16, lanes), jnp.float32),
            pltpu.VMEM((3, length_x + 4, length_z + 8, lanes), jnp.float32),
            pltpu.VMEM(velocity.shape, jnp.float32),
            pltpu.SemaphoreType.DMA((len(CHUNKS),)),
            pltpu.SemaphoreType.DMA((5,)),
            pltpu.SemaphoreType.DMA((1,)),
        ],
        compiler_params=pltpu.CompilerParams(vmem_limit_bytes=36 * 2**20),
        name="step_gram",
    )(velocity, *halos, weights, basis, stored)


def shift(part, axis, step):
    count = lax.axis_size(axis)
    return lax.ppermute(part, axis, [(i, (i + step) % count) for i in range(count)])


def exchange(velocity):
    left = shift(velocity[:, -4:], "gx", 1)
    right = shift(velocity[:, :4], "gx", -1)
    back, front = lax.optimization_barrier((velocity[:, :, -4:], velocity[:, :, :4]))
    back = jnp.concatenate([left[:, 2:, -4:], back, right[:, :2, -4:]], axis=1)
    front = jnp.concatenate([left[:, 2:, :4], front, right[:, :2, :4]], axis=1)
    behind = shift(back, "gy", 1)
    ahead = shift(front, "gy", -1)
    return left, right, behind, ahead


def wall_rows(points):
    up, down, here, curve_down, curve_here, curve_up = wall_weights(points)
    lane = jnp.arange(points)
    has_up = lane < points - 1
    has_down = lane > 0
    return jnp.stack(
        [
            jnp.where(has_up, up, 0.0),
            jnp.where(has_down, down, 0.0),
            here,
            VISCOSITY * jnp.where(has_up, curve_down, 0.0),
            VISCOSITY * curve_here,
            VISCOSITY * jnp.where(has_down, curve_up, 0.0),
            jnp.zeros_like(here),
            jnp.zeros_like(here),
        ]
    )


def swap_cores(part, count):
    return lax.ppermute(part, "gy", [(i, i ^ 1) for i in range(count)])


def ring_sum(part, axis, count, stride):
    def target(i, d):
        place = (i // stride) % 4
        return i + ((place + d) % 4 - place) * stride

    moved = [
        lax.ppermute(part, axis, [(i, target(i, d)) for i in range(count)]) for d in (1, 2, 3)
    ]
    return (part + moved[1]) + (moved[0] + moved[2])


def total_gram(gram):
    count = lax.axis_size("gy")
    half = gram.shape[0] // 2
    core = lax.axis_index("gy") % 2
    mine = lax.dynamic_slice_in_dim(gram, core * half, half, 0)
    other = lax.dynamic_slice_in_dim(gram, (1 - core) * half, half, 0)
    part = mine + swap_cores(other, count)
    part = ring_sum(part, "gy", count, 2)
    part = ring_sum(part, "gy", count, 8)
    part = ring_sum(part, "gx", 4, 1)
    rest = swap_cores(part, count)
    low = jnp.where(core == 0, part, rest)
    high = jnp.where(core == 0, rest, part)
    return jnp.concatenate([low, high], 0)


PANEL = 16


def factor_kernel(gram_ref, factor_ref, work):
    size = gram_ref.shape[0]
    work[...] = gram_ref[...]
    row = lax.broadcasted_iota(jnp.int32, (PANEL, size), 0)
    lane = lax.broadcasted_iota(jnp.int32, (PANEL, size), 1)
    for begin in range(0, size, PANEL):
        end = begin + PANEL
        rows = work[begin:end, :]
        columns = [
            jnp.broadcast_to(rows[:, begin + k : begin + k + 1], (PANEL, size))
            for k in range(PANEL)
        ]
        scales = jnp.zeros((PANEL, size), jnp.float32)
        for j in range(PANEL):
            scale = lax.rsqrt(columns[j][j : j + 1, :])
            below = jnp.where(row > j, columns[j] * scale, 0.0)
            for k in range(j + 1, PANEL):
                columns[k] = columns[k] - below * (columns[k][j : j + 1, :] * scale)
            rows = rows - below * (rows[j : j + 1, :] * scale)
            scales = jnp.where(row == j, jnp.broadcast_to(scale, (PANEL, size)), scales)
        done = jnp.where(lane >= row + begin, rows * scales, 0.0)
        factor_ref[begin:end, :] = done
        if end < size:
            high = done.astype(jnp.bfloat16)
            left = done - high.astype(jnp.float32)
            mid = left.astype(jnp.bfloat16)
            low = (left - mid.astype(jnp.float32)).astype(jnp.bfloat16)
            product = lax.dot_general(
                jnp.concatenate([high, high, mid, high, low, mid], 0),
                jnp.concatenate([high, mid, high, low, high, mid], 0),
                (((0,), (0,)), ((), ())),
                preferred_element_type=jnp.float32,
            )
            work[end:, :] = work[end:, :] - product[end:, :]


def upper_factor(gram):
    return pl.pallas_call(
        factor_kernel,
        out_shape=jax.ShapeDtypeStruct(gram.shape, jnp.float32),
        in_specs=[pl.BlockSpec(memory_space=pltpu.VMEM)],
        out_specs=pl.BlockSpec(memory_space=pltpu.VMEM),
        scratch_shapes=[pltpu.VMEM(gram.shape, jnp.float32)],
        compiler_params=pltpu.CompilerParams(vmem_limit_bytes=8 * 2**20),
        name="upper_factor",
    )(gram)


def local(velocity, basis, snapshots):
    total_rows = (
        3.0
        * velocity.shape[1]
        * lax.axis_size("gx")
        * velocity.shape[2]
        * lax.axis_size("gy")
        * velocity.shape[3]
    )
    halos = exchange(velocity)
    weights = wall_rows(velocity.shape[3])
    advanced, gram = step_and_gram(velocity, halos, weights, basis, snapshots, 1.0 / total_rows)
    factor = upper_factor(total_gram(gram))
    return (advanced, factor)


def solution(mesh):
    return jax.shard_map(
        local,
        mesh=mesh,
        in_specs=(
            P(None, "gx", "gy", None),
            P(None, None, "gx", "gy", None),
            P(None, None, "gx", "gy", None),
        ),
        out_specs=(P(None, "gx", "gy", None), P()),
        check_vma=False,
    )
```

```python
import functools
import math

import jax
import jax.numpy as jnp
from jax import lax
from jax.experimental import pallas as pl
from jax.experimental.pallas import tpu as pltpu
from jax.sharding import PartitionSpec as P

TIME_STEP = 0.0002
VISCOSITY = 0.005
STEP_X = 0.0123
STEP_Z = 0.0092
STRETCH = 2.0


def wall_weights(points):
    positions = jnp.arange(points + 2, dtype=jnp.float32)
    nodes = -jnp.tanh(STRETCH * (1.0 - 2.0 * positions / (points + 1))) / math.tanh(STRETCH)
    below = nodes[1:-1] - nodes[:-2]
    above = nodes[2:] - nodes[1:-1]
    spread = above * below * (above + below)
    return (
        below * below / spread,
        -(above * above) / spread,
        (above * above - below * below) / spread,
        2.0 * below / spread,
        -2.0 * (above + below) / spread,
        2.0 * above / spread,
    )


def tendency(field, place, first, count, weights):
    def rows(c, dx, dz):
        return field[c, place + dx, pl.ds(first + dz, count), :]

    centers = [rows(c, 0, 0) for c in range(3)]
    lanes = centers[0].shape[1]
    along_x = centers[0] * (1.0 / (12.0 * STEP_X))
    along_z = centers[2] * (1.0 / (12.0 * STEP_Z))
    results = []
    for c in range(3):
        center = centers[c]
        x2, x1, x_1, x_2 = (rows(c, d, 0) for d in (2, 1, -1, -2))
        z2, z1, z_1, z_2 = (rows(c, 0, d) for d in (2, 1, -1, -2))
        upper = pltpu.roll(center, lanes - 1, 1)
        lower = pltpu.roll(center, 1, 1)
        slope_x = 8.0 * (x1 - x_1) - (x2 - x_2)
        slope_z = 8.0 * (z1 - z_1) - (z2 - z_2)
        slope_y = weights[0] * upper + weights[1] * lower + weights[2] * center
        curve_x = 16.0 * (x1 + x_1) - (x2 + x_2) - 30.0 * center
        curve_z = 16.0 * (z1 + z_1) - (z2 + z_2) - 30.0 * center
        curve_y = weights[3] * upper + weights[4] * center + weights[5] * lower
        carried = along_x * slope_x + centers[1] * slope_y + along_z * slope_z
        spread = (
            curve_x * (VISCOSITY / (12.0 * STEP_X * STEP_X))
            + curve_z * (VISCOSITY / (12.0 * STEP_Z * STEP_Z))
            + curve_y
        )
        results.append((center, spread - carried))
    return results


PACKED_ROWS = 80


def pack_gram(gram, packed_ref):
    half = gram.shape[0] // 2
    first, second = gram[:half], gram[half:]
    row = lax.broadcasted_iota(jnp.int32, first.shape, 0)
    lane = lax.broadcasted_iota(jnp.int32, first.shape, 1)
    packed_ref[0:half, :] = jnp.where(lane < row, pltpu.roll(second, half, 1), first)
    diagonal = jnp.sum(jnp.where(lane == row + half, second, 0.0), axis=0, keepdims=True)
    packed_ref[half:, :] = jnp.broadcast_to(diagonal, (PACKED_ROWS - half, gram.shape[1]))


def unpack_gram(packed_ref, gram_ref):
    size = gram_ref.shape[0]
    half = size // 2
    kept = packed_ref[0:half, :]
    turned = jnp.concatenate([kept, jnp.zeros_like(kept)], 0).T[0:half]
    row = lax.broadcasted_iota(jnp.int32, kept.shape, 0)
    lane = lax.broadcasted_iota(jnp.int32, kept.shape, 1)
    gram_ref[0:half, :] = jnp.where(lane < row, turned, kept)
    second = pltpu.roll(jnp.where(lane < row, kept, turned), half, 1)
    diagonal = jnp.broadcast_to(packed_ref[half : half + 1, :], kept.shape)
    gram_ref[half:, :] = jnp.where(lane == row + half, diagonal, second)


CHUNKS = (160, 128, 96)
MXU_STEP = 32


def step_kernel(
    scale,
    velocity_ref,
    left_ref,
    right_ref,
    behind_ref,
    ahead_ref,
    weights_ref,
    basis_ref,
    stored_ref,
    advanced_ref,
    packed_ref,
    block,
    wide,
    folded,
    field,
    section,
    advanced,
    sems,
    halo_sems,
    out_sem,
):
    n_basis = basis_ref.shape[0]
    n_stored = stored_ref.shape[0]
    length_x, length_z = velocity_ref.shape[1:3]
    starts = [sum(CHUNKS[:q]) for q in range(len(CHUNKS))]

    halos = [
        pltpu.make_async_copy(source, target, halo_sems.at[i])
        for i, (source, target) in enumerate(
            (
                (velocity_ref, field.at[:, pl.ds(4, length_x), pl.ds(4, length_z)]),
                (left_ref, field.at[:, pl.ds(0, 4), pl.ds(4, length_z)]),
                (right_ref, field.at[:, pl.ds(4 + length_x, 4), pl.ds(4, length_z)]),
                (behind_ref, field.at[:, pl.ds(2, 4 + length_x), pl.ds(0, 4)]),
                (ahead_ref, field.at[:, pl.ds(2, 4 + length_x), pl.ds(4 + length_z, 4)]),
            )
        )
    ]
    for halo in halos:
        halo.start()

    def issue(q):
        span = pl.ds(starts[q], CHUNKS[q])

        def send(source, column):
            pltpu.make_async_copy(
                source.at[span], block.at[span, pl.ds(pl.multiple_of(2 * column, 2), 2)], sems.at[q]
            ).start()

        def from_basis(c, carry):
            send(basis_ref.at[c], c)
            return carry

        def from_stored(c, carry):
            send(stored_ref.at[c], n_basis + c)
            return carry

        lax.fori_loop(0, n_basis, from_basis, 0, unroll=8)
        lax.fori_loop(0, n_stored, from_stored, 0, unroll=9)

    for q in range(len(CHUNKS)):
        issue(q)
    for halo in halos:
        halo.wait()

    weights = [weights_ref[i : i + 1, :] for i in range(6)]

    @pl.loop(0, length_x + 4)
    def _(x):
        for c, (center, change) in enumerate(tendency(field, x + 2, 2, length_z + 8, weights)):
            section[c, x, pl.ds(0, length_z + 8), :] = center + TIME_STEP * change

    last = 2 * (n_basis + n_stored)

    @pl.loop(0, length_x)
    def _(x):
        for c, (center, change) in enumerate(tendency(section, x + 2, 2, length_z, weights)):
            begin = field[c, x + 4, pl.ds(4, length_z), :]
            end = 0.5 * (begin + center + TIME_STEP * change)
            advanced[c, x] = end
            rounded = end.astype(jnp.bfloat16)
            pair = (c * length_x + x) * (length_z // 2)
            for j in range(length_z // 2):
                block[pair + j, last : last + 2, :] = rounded[2 * j : 2 * j + 2, :]

    leave = pltpu.make_async_copy(advanced, advanced_ref, out_sem.at[0])
    leave.start()

    def body(acc0, acc1):
        accs = (acc0, acc1)
        for q in range(len(CHUNKS)):
            arrived = block.at[pl.ds(starts[q], CHUNKS[q]), pl.ds(0, last)]
            pltpu.make_async_copy(arrived, arrived, sems.at[q]).wait()

            @pl.loop(0, CHUNKS[q] // MXU_STEP)
            def _(t):
                base = starts[q] + t * MXU_STEP
                for u in range(MXU_STEP // 2):
                    unit = u % 2
                    register = (u // 2) % 2
                    rows = jnp.concatenate([block[base + 2 * u], block[base + 2 * u + 1]], axis=1)
                    pltpu.matmul_push_rhs(rows, register, unit, transpose=True)
                    pltpu.matmul_acc_lhs(accs[unit], rows, load_staged_rhs=register)

        total = pltpu.matmul_pop(acc0) + pltpu.matmul_pop(acc1)
        for h in range(2):
            wide[h] = total[:, 128 * h : 128 * (h + 1)]

    pl.run_scoped(
        body, pltpu.ACC(0)((256, 256), jnp.float32), pltpu.ACC(1)((256, 256), jnp.float32)
    )
    lane = lax.broadcasted_iota(jnp.int32, (128, 128), 1)
    for h in range(2):
        even = wide[h, pl.ds(0, 128, stride=2), :]
        odd = wide[h, pl.ds(1, 128, stride=2), :]
        folded[128 * h : 128 * (h + 1)] = (jnp.where(lane % 2 == 0, even, odd) * scale).T
    gram = folded[pl.ds(0, 128, stride=2), :] + folded[pl.ds(1, 128, stride=2), :]
    pack_gram(gram, packed_ref)
    leave.wait()


def pair_rows(fields):
    return fields.reshape(fields.shape[0], -1, 2, fields.shape[-1])


def step_and_gram(velocity, halos, weights, basis, stored, scale):
    basis = pltpu.with_memory_space_constraint(pair_rows(basis), pltpu.HBM)
    stored = pltpu.with_memory_space_constraint(pair_rows(stored), pltpu.HBM)
    velocity = pltpu.with_memory_space_constraint(velocity, pltpu.HBM)
    length_x, length_z, lanes = velocity.shape[1:]
    hbm = pl.BlockSpec(memory_space=pltpu.HBM)
    free = pl.BlockSpec(memory_space=pl.ANY)
    vmem = pl.BlockSpec(memory_space=pltpu.VMEM)
    return pl.pallas_call(
        functools.partial(step_kernel, scale),
        out_shape=(
            jax.ShapeDtypeStruct(velocity.shape, jnp.float32),
            jax.ShapeDtypeStruct((PACKED_ROWS, 128), jnp.float32),
        ),
        in_specs=[hbm, free, free, free, free, vmem, hbm, hbm],
        out_specs=(hbm, vmem),
        scratch_shapes=[
            pltpu.VMEM((basis.shape[1], 256, lanes), jnp.bfloat16),
            pltpu.VMEM((2, 256, 128), jnp.float32),
            pltpu.VMEM((256, 128), jnp.float32),
            pltpu.VMEM((3, length_x + 8, length_z + 16, lanes), jnp.float32),
            pltpu.VMEM((3, length_x + 4, length_z + 8, lanes), jnp.float32),
            pltpu.VMEM(velocity.shape, jnp.float32),
            pltpu.SemaphoreType.DMA((len(CHUNKS),)),
            pltpu.SemaphoreType.DMA((5,)),
            pltpu.SemaphoreType.DMA((1,)),
        ],
        compiler_params=pltpu.CompilerParams(vmem_limit_bytes=36 * 2**20),
        name="step_gram",
    )(velocity, *halos, weights, basis, stored)


def shift(part, axis, step):
    count = lax.axis_size(axis)
    return lax.ppermute(part, axis, [(i, (i + step) % count) for i in range(count)])


def exchange(velocity):
    left = shift(velocity[:, -4:], "gx", 1)
    right = shift(velocity[:, :4], "gx", -1)
    back, front = lax.optimization_barrier((velocity[:, :, -4:], velocity[:, :, :4]))
    back = jnp.concatenate([left[:, 2:, -4:], back, right[:, :2, -4:]], axis=1)
    front = jnp.concatenate([left[:, 2:, :4], front, right[:, :2, :4]], axis=1)
    behind = shift(back, "gy", 1)
    ahead = shift(front, "gy", -1)
    return left, right, behind, ahead


def wall_rows(points):
    up, down, here, curve_down, curve_here, curve_up = wall_weights(points)
    lane = jnp.arange(points)
    has_up = lane < points - 1
    has_down = lane > 0
    return jnp.stack(
        [
            jnp.where(has_up, up, 0.0),
            jnp.where(has_down, down, 0.0),
            here,
            VISCOSITY * jnp.where(has_up, curve_down, 0.0),
            VISCOSITY * curve_here,
            VISCOSITY * jnp.where(has_down, curve_up, 0.0),
            jnp.zeros_like(here),
            jnp.zeros_like(here),
        ]
    )


def swap_cores(part, count):
    return lax.ppermute(part, "gy", [(i, i ^ 1) for i in range(count)])


def group_sum(part, axis, members, groups=None):
    copies = jnp.broadcast_to(part[None], (members, *part.shape))
    return lax.all_to_all(copies, axis, 0, 0, axis_index_groups=groups).sum(0)


def total_gram(packed):
    count = lax.axis_size("gy")
    half = packed.shape[0] // 2
    core = lax.axis_index("gy") % 2
    mine = lax.dynamic_slice_in_dim(packed, core * half, half, 0)
    other = lax.dynamic_slice_in_dim(packed, (1 - core) * half, half, 0)
    part = mine + swap_cores(other, count)
    part = group_sum(part, "gy", count // 2, [list(range(c, count, 2)) for c in range(2)])
    part = group_sum(part, "gx", lax.axis_size("gx"))
    rest = swap_cores(part, count)
    low = jnp.where(core == 0, part, rest)
    high = jnp.where(core == 0, rest, part)
    return jnp.concatenate([low, high], 0)


PANEL = 16


def factor_kernel(packed_ref, factor_ref, work):
    size = work.shape[0]
    unpack_gram(packed_ref, work)
    row = lax.broadcasted_iota(jnp.int32, (PANEL, size), 0)
    lane = lax.broadcasted_iota(jnp.int32, (PANEL, size), 1)
    for begin in range(0, size, PANEL):
        end = begin + PANEL
        rows = work[begin:end, :]
        columns = [
            jnp.broadcast_to(rows[:, begin + k : begin + k + 1], (PANEL, size))
            for k in range(PANEL)
        ]
        scales = jnp.zeros((PANEL, size), jnp.float32)
        for j in range(PANEL):
            scale = lax.rsqrt(columns[j][j : j + 1, :])
            below = jnp.where(row > j, columns[j] * scale, 0.0)
            for k in range(j + 1, PANEL):
                columns[k] = columns[k] - below * (columns[k][j : j + 1, :] * scale)
            rows = rows - below * (rows[j : j + 1, :] * scale)
            scales = jnp.where(row == j, jnp.broadcast_to(scale, (PANEL, size)), scales)
        done = jnp.where(lane >= row + begin, rows * scales, 0.0)
        factor_ref[begin:end, :] = done
        if end < size:
            high = done.astype(jnp.bfloat16)
            left = done - high.astype(jnp.float32)
            mid = left.astype(jnp.bfloat16)
            low = (left - mid.astype(jnp.float32)).astype(jnp.bfloat16)
            product = lax.dot_general(
                jnp.concatenate([high, high, mid, high, low, mid], 0),
                jnp.concatenate([high, mid, high, low, high, mid], 0),
                (((0,), (0,)), ((), ())),
                preferred_element_type=jnp.float32,
            )
            work[end:, :] = work[end:, :] - product[end:, :]


def upper_factor(packed):
    shape = (packed.shape[1], packed.shape[1])
    return pl.pallas_call(
        factor_kernel,
        out_shape=jax.ShapeDtypeStruct(shape, jnp.float32),
        in_specs=[pl.BlockSpec(memory_space=pltpu.VMEM)],
        out_specs=pl.BlockSpec(memory_space=pltpu.VMEM),
        scratch_shapes=[pltpu.VMEM(shape, jnp.float32)],
        compiler_params=pltpu.CompilerParams(vmem_limit_bytes=8 * 2**20),
        name="upper_factor",
    )(packed)


def local(velocity, basis, snapshots):
    total_rows = (
        3.0
        * velocity.shape[1]
        * lax.axis_size("gx")
        * velocity.shape[2]
        * lax.axis_size("gy")
        * velocity.shape[3]
    )
    halos = exchange(velocity)
    weights = wall_rows(velocity.shape[3])
    advanced, packed = step_and_gram(velocity, halos, weights, basis, snapshots, 1.0 / total_rows)
    factor = upper_factor(total_gram(packed))
    return (advanced, factor)


def solution(mesh):
    return jax.shard_map(
        local,
        mesh=mesh,
        in_specs=(
            P(None, "gx", "gy", None),
            P(None, None, "gx", "gy", None),
            P(None, None, "gx", "gy", None),
        ),
        out_specs=(P(None, "gx", "gy", None), P()),
        check_vma=False,
    )
```

```python
import functools
import math

import jax
import jax.numpy as jnp
from jax import lax
from jax.experimental import pallas as pl
from jax.experimental.pallas import tpu as pltpu
from jax.sharding import PartitionSpec as P


TIME_STEP = 0.0002
VISCOSITY = 0.005
STEP_X = 0.0123
STEP_Z = 0.0092
STRETCH = 2.0


def wall_weights(points):
    positions = jnp.arange(points + 2, dtype=jnp.float32)
    nodes = -jnp.tanh(STRETCH * (1.0 - 2.0 * positions / (points + 1))) / math.tanh(STRETCH)
    below = nodes[1:-1] - nodes[:-2]
    above = nodes[2:] - nodes[1:-1]
    spread = above * below * (above + below)
    return (
        below * below / spread,
        -(above * above) / spread,
        (above * above - below * below) / spread,
        2.0 * below / spread,
        -2.0 * (above + below) / spread,
        2.0 * above / spread,
    )


def tendency(field, place, first, count, weights):
    def rows(c, dx, dz):
        return field[c, place + dx, pl.ds(first + dz, count), :]

    centers = [rows(c, 0, 0) for c in range(3)]
    lanes = centers[0].shape[1]
    along_x = centers[0] * (1.0 / (12.0 * STEP_X))
    along_z = centers[2] * (1.0 / (12.0 * STEP_Z))
    results = []
    for c in range(3):
        center = centers[c]
        x2, x1, x_1, x_2 = (rows(c, d, 0) for d in (2, 1, -1, -2))
        z2, z1, z_1, z_2 = (rows(c, 0, d) for d in (2, 1, -1, -2))
        upper = pltpu.roll(center, lanes - 1, 1)
        lower = pltpu.roll(center, 1, 1)
        slope_x = 8.0 * (x1 - x_1) - (x2 - x_2)
        slope_z = 8.0 * (z1 - z_1) - (z2 - z_2)
        slope_y = weights[0] * upper + weights[1] * lower + weights[2] * center
        curve_x = 16.0 * (x1 + x_1) - (x2 + x_2) - 30.0 * center
        curve_z = 16.0 * (z1 + z_1) - (z2 + z_2) - 30.0 * center
        curve_y = weights[3] * upper + weights[4] * center + weights[5] * lower
        carried = along_x * slope_x + centers[1] * slope_y + along_z * slope_z
        spread = (
            curve_x * (VISCOSITY / (12.0 * STEP_X * STEP_X))
            + curve_z * (VISCOSITY / (12.0 * STEP_Z * STEP_Z))
            + curve_y
        )
        results.append((center, spread - carried))
    return results


PACKED_ROWS = 80


def pack_gram(gram, packed_ref):
    half = gram.shape[0] // 2
    first, second = gram[:half], gram[half:]
    row = lax.broadcasted_iota(jnp.int32, first.shape, 0)
    lane = lax.broadcasted_iota(jnp.int32, first.shape, 1)
    packed_ref[0:half, :] = jnp.where(lane < row, pltpu.roll(second, half, 1), first)
    diagonal = jnp.sum(jnp.where(lane == row + half, second, 0.0), axis=0, keepdims=True)
    packed_ref[half:, :] = jnp.broadcast_to(diagonal, (PACKED_ROWS - half, gram.shape[1]))


def unpack_gram(packed_ref, gram_ref):
    size = gram_ref.shape[0]
    half = size // 2
    kept = packed_ref[0:half, :]
    turned = jnp.concatenate([kept, jnp.zeros_like(kept)], 0).T[0:half]
    row = lax.broadcasted_iota(jnp.int32, kept.shape, 0)
    lane = lax.broadcasted_iota(jnp.int32, kept.shape, 1)
    gram_ref[0:half, :] = jnp.where(lane < row, turned, kept)
    second = pltpu.roll(jnp.where(lane < row, kept, turned), half, 1)
    diagonal = jnp.broadcast_to(packed_ref[half : half + 1, :], kept.shape)
    gram_ref[half:, :] = jnp.where(lane == row + half, diagonal, second)


CHUNKS = (128, 128, 128)
MXU_STEP = 32


def step_kernel(
    scale,
    velocity_ref,
    left_ref,
    right_ref,
    behind_ref,
    ahead_ref,
    weights_ref,
    basis_ref,
    stored_ref,
    advanced_ref,
    packed_ref,
    block,
    wide,
    folded,
    field,
    section,
    advanced,
    sems,
    halo_sems,
    out_sem,
):
    n_basis = basis_ref.shape[0]
    n_stored = stored_ref.shape[0]
    length_x, length_z = velocity_ref.shape[1:3]
    starts = [sum(CHUNKS[:q]) for q in range(len(CHUNKS))]

    halos = [
        pltpu.make_async_copy(source, target, halo_sems.at[i])
        for i, (source, target) in enumerate(
            (
                (velocity_ref, field.at[:, pl.ds(4, length_x), pl.ds(4, length_z)]),
                (left_ref, field.at[:, pl.ds(0, 4), pl.ds(4, length_z)]),
                (right_ref, field.at[:, pl.ds(4 + length_x, 4), pl.ds(4, length_z)]),
                (behind_ref, field.at[:, pl.ds(2, 4 + length_x), pl.ds(0, 4)]),
                (ahead_ref, field.at[:, pl.ds(2, 4 + length_x), pl.ds(4 + length_z, 4)]),
            )
        )
    ]
    for halo in halos:
        halo.start()

    def send(q, source, column, place):
        span = pl.ds(starts[q], CHUNKS[q])
        pltpu.make_async_copy(
            source.at[column, span],
            block.at[span, pl.ds(pl.multiple_of(2 * (place + column), 2), 2)],
            sems.at[q],
        ).start()

    def issue_part(q, part, parts):
        for source, place in ((basis_ref, 0), (stored_ref, n_basis)):
            share = source.shape[0] // parts
            for i in range(share):
                send(q, source, part * share + i, place)

    def issue_rest(q, parts):
        for source, place in ((basis_ref, 0), (stored_ref, n_basis)):
            for column in range(source.shape[0] // parts * parts, source.shape[0]):
                send(q, source, column, place)

    def section_plane(x):
        for c, (center, change) in enumerate(tendency(field, x + 2, 2, length_z + 8, weights)):
            section[c, x, pl.ds(0, length_z + 8), :] = center + TIME_STEP * change

    @pl.loop(0, 8)
    def _(part):
        issue_part(0, part, 8)

    issue_rest(0, 8)
    for halo in halos:
        halo.wait()

    weights = [weights_ref[i : i + 1, :] for i in range(6)]

    @pl.loop(0, length_x)
    def _(x):
        issue_part(1, x, length_x)
        section_plane(x)

    issue_rest(1, length_x)

    @pl.loop(length_x, length_x + 4)
    def _(x):
        section_plane(x)

    last = 2 * (n_basis + n_stored)

    @pl.loop(0, length_x)
    def _(x):
        issue_part(2, x, length_x)
        for c, (center, change) in enumerate(tendency(section, x + 2, 2, length_z, weights)):
            begin = field[c, x + 4, pl.ds(4, length_z), :]
            end = 0.5 * (begin + center + TIME_STEP * change)
            advanced[c, x] = end
            rounded = end.astype(jnp.bfloat16)
            pair = (c * length_x + x) * (length_z // 2)
            for j in range(length_z // 2):
                block[pair + j, last : last + 2, :] = rounded[2 * j : 2 * j + 2, :]

    issue_rest(2, length_x)

    leave = pltpu.make_async_copy(advanced, advanced_ref, out_sem.at[0])
    leave.start()

    def body(acc0, acc1):
        accs = (acc0, acc1)
        for q in range(len(CHUNKS)):
            arrived = block.at[pl.ds(starts[q], CHUNKS[q]), pl.ds(0, last)]
            pltpu.make_async_copy(arrived, arrived, sems.at[q]).wait()

            @pl.loop(0, CHUNKS[q] // MXU_STEP)
            def _(t):
                base = starts[q] + t * MXU_STEP
                for u in range(MXU_STEP // 2):
                    unit = u % 2
                    register = (u // 2) % 2
                    rows = jnp.concatenate([block[base + 2 * u], block[base + 2 * u + 1]], axis=1)
                    pltpu.matmul_push_rhs(rows, register, unit, transpose=True)
                    pltpu.matmul_acc_lhs(accs[unit], rows, load_staged_rhs=register)

        total = pltpu.matmul_pop(acc0) + pltpu.matmul_pop(acc1)
        for h in range(2):
            wide[h] = total[:, 128 * h : 128 * (h + 1)]

    pl.run_scoped(
        body, pltpu.ACC(0)((256, 256), jnp.float32), pltpu.ACC(1)((256, 256), jnp.float32)
    )
    lane = lax.broadcasted_iota(jnp.int32, (128, 128), 1)
    for h in range(2):
        even = wide[h, pl.ds(0, 128, stride=2), :]
        odd = wide[h, pl.ds(1, 128, stride=2), :]
        folded[128 * h : 128 * (h + 1)] = (jnp.where(lane % 2 == 0, even, odd) * scale).T
    gram = folded[pl.ds(0, 128, stride=2), :] + folded[pl.ds(1, 128, stride=2), :]
    pack_gram(gram, packed_ref)
    leave.wait()


def pair_rows(fields):
    return fields.reshape(fields.shape[0], -1, 2, fields.shape[-1])


def step_and_gram(velocity, halos, weights, basis, stored, scale):
    basis = pltpu.with_memory_space_constraint(pair_rows(basis), pltpu.HBM)
    stored = pltpu.with_memory_space_constraint(pair_rows(stored), pltpu.HBM)
    velocity = pltpu.with_memory_space_constraint(velocity, pltpu.HBM)
    length_x, length_z, lanes = velocity.shape[1:]
    hbm = pl.BlockSpec(memory_space=pltpu.HBM)
    free = pl.BlockSpec(memory_space=pl.ANY)
    vmem = pl.BlockSpec(memory_space=pltpu.VMEM)
    return pl.pallas_call(
        functools.partial(step_kernel, scale),
        out_shape=(
            jax.ShapeDtypeStruct(velocity.shape, jnp.float32),
            jax.ShapeDtypeStruct((PACKED_ROWS, 128), jnp.float32),
        ),
        in_specs=[hbm, free, free, free, free, vmem, hbm, hbm],
        out_specs=(hbm, vmem),
        scratch_shapes=[
            pltpu.VMEM((basis.shape[1], 256, lanes), jnp.bfloat16),
            pltpu.VMEM((2, 256, 128), jnp.float32),
            pltpu.VMEM((256, 128), jnp.float32),
            pltpu.VMEM((3, length_x + 8, length_z + 16, lanes), jnp.float32),
            pltpu.VMEM((3, length_x + 4, length_z + 8, lanes), jnp.float32),
            pltpu.VMEM(velocity.shape, jnp.float32),
            pltpu.SemaphoreType.DMA((len(CHUNKS),)),
            pltpu.SemaphoreType.DMA((5,)),
            pltpu.SemaphoreType.DMA((1,)),
        ],
        compiler_params=pltpu.CompilerParams(vmem_limit_bytes=36 * 2**20),
        name="step_gram",
    )(velocity, *halos, weights, basis, stored)


def shift(part, axis, step):
    count = lax.axis_size(axis)
    return lax.ppermute(part, axis, [(i, (i + step) % count) for i in range(count)])


def exchange(velocity):
    left = shift(velocity[:, -4:], "gx", 1)
    right = shift(velocity[:, :4], "gx", -1)
    back, front = lax.optimization_barrier((velocity[:, :, -4:], velocity[:, :, :4]))
    back = jnp.concatenate([left[:, 2:, -4:], back, right[:, :2, -4:]], axis=1)
    front = jnp.concatenate([left[:, 2:, :4], front, right[:, :2, :4]], axis=1)
    behind = shift(back, "gy", 1)
    ahead = shift(front, "gy", -1)
    return left, right, behind, ahead


def wall_rows(points):
    up, down, here, curve_down, curve_here, curve_up = wall_weights(points)
    lane = jnp.arange(points)
    has_up = lane < points - 1
    has_down = lane > 0
    return jnp.stack(
        [
            jnp.where(has_up, up, 0.0),
            jnp.where(has_down, down, 0.0),
            here,
            VISCOSITY * jnp.where(has_up, curve_down, 0.0),
            VISCOSITY * curve_here,
            VISCOSITY * jnp.where(has_down, curve_up, 0.0),
            jnp.zeros_like(here),
            jnp.zeros_like(here),
        ]
    )


def swap_cores(part, count):
    return lax.ppermute(part, "gy", [(i, i ^ 1) for i in range(count)])


def group_sum(part, axis, members, groups=None):
    copies = jnp.broadcast_to(part[None], (members, *part.shape))
    return lax.all_to_all(copies, axis, 0, 0, axis_index_groups=groups).sum(0)


def total_gram(packed):
    count = lax.axis_size("gy")
    half = packed.shape[0] // 2
    core = lax.axis_index("gy") % 2
    mine = lax.dynamic_slice_in_dim(packed, core * half, half, 0)
    other = lax.dynamic_slice_in_dim(packed, (1 - core) * half, half, 0)
    part = mine + swap_cores(other, count)
    part = group_sum(part, "gy", count // 2, [list(range(c, count, 2)) for c in range(2)])
    part = group_sum(part, "gx", lax.axis_size("gx"))
    rest = swap_cores(part, count)
    low = jnp.where(core == 0, part, rest)
    high = jnp.where(core == 0, rest, part)
    return jnp.concatenate([low, high], 0)


PANEL = 16


def factor_kernel(packed_ref, factor_ref, work):
    size = work.shape[0]
    unpack_gram(packed_ref, work)
    row = lax.broadcasted_iota(jnp.int32, (PANEL, size), 0)
    lane = lax.broadcasted_iota(jnp.int32, (PANEL, size), 1)
    for begin in range(0, size, PANEL):
        end = begin + PANEL
        rows = work[begin:end, :]
        columns = [
            jnp.broadcast_to(rows[:, begin + k : begin + k + 1], (PANEL, size))
            for k in range(PANEL)
        ]
        scales = jnp.zeros((PANEL, size), jnp.float32)
        for j in range(PANEL):
            scale = lax.rsqrt(columns[j][j : j + 1, :])
            below = jnp.where(row > j, columns[j] * scale, 0.0)
            for k in range(j + 1, PANEL):
                columns[k] = columns[k] - below * (columns[k][j : j + 1, :] * scale)
            rows = rows - below * (rows[j : j + 1, :] * scale)
            scales = jnp.where(row == j, jnp.broadcast_to(scale, (PANEL, size)), scales)
        done = jnp.where(lane >= row + begin, rows * scales, 0.0)
        factor_ref[begin:end, :] = done
        if end < size:
            high = done.astype(jnp.bfloat16)
            left = done - high.astype(jnp.float32)
            mid = left.astype(jnp.bfloat16)
            low = (left - mid.astype(jnp.float32)).astype(jnp.bfloat16)
            product = lax.dot_general(
                jnp.concatenate([high, high, mid, high, low, mid], 0),
                jnp.concatenate([high, mid, high, low, high, mid], 0),
                (((0,), (0,)), ((), ())),
                preferred_element_type=jnp.float32,
            )
            work[end:, :] = work[end:, :] - product[end:, :]


def upper_factor(packed):
    shape = (packed.shape[1], packed.shape[1])
    return pl.pallas_call(
        factor_kernel,
        out_shape=jax.ShapeDtypeStruct(shape, jnp.float32),
        in_specs=[pl.BlockSpec(memory_space=pltpu.VMEM)],
        out_specs=pl.BlockSpec(memory_space=pltpu.VMEM),
        scratch_shapes=[pltpu.VMEM(shape, jnp.float32)],
        compiler_params=pltpu.CompilerParams(vmem_limit_bytes=8 * 2**20),
        name="upper_factor",
    )(packed)


def local(velocity, basis, snapshots):
    total_rows = (
        3.0
        * velocity.shape[1]
        * lax.axis_size("gx")
        * velocity.shape[2]
        * lax.axis_size("gy")
        * velocity.shape[3]
    )
    halos = exchange(velocity)
    weights = wall_rows(velocity.shape[3])
    advanced, packed = step_and_gram(velocity, halos, weights, basis, snapshots, 1.0 / total_rows)
    factor = upper_factor(total_gram(packed))
    return (advanced, factor)


def solution(mesh):
    return jax.shard_map(
        local,
        mesh=mesh,
        in_specs=(
            P(None, "gx", "gy", None),
            P(None, None, "gx", "gy", None),
            P(None, None, "gx", "gy", None),
        ),
        out_specs=(P(None, "gx", "gy", None), P()),
        check_vma=False,
    )
```

```python
import functools
import math

import jax
import jax.numpy as jnp
from jax import lax
from jax.experimental import pallas as pl
from jax.experimental.pallas import tpu as pltpu
from jax.sharding import PartitionSpec as P


TIME_STEP = 0.0002
VISCOSITY = 0.005
STEP_X = 0.0123
STEP_Z = 0.0092
STRETCH = 2.0


def wall_weights(points):
    positions = jnp.arange(points + 2, dtype=jnp.float32)
    nodes = -jnp.tanh(STRETCH * (1.0 - 2.0 * positions / (points + 1))) / math.tanh(STRETCH)
    below = nodes[1:-1] - nodes[:-2]
    above = nodes[2:] - nodes[1:-1]
    spread = above * below * (above + below)
    return (
        below * below / spread,
        -(above * above) / spread,
        (above * above - below * below) / spread,
        2.0 * below / spread,
        -2.0 * (above + below) / spread,
        2.0 * above / spread,
    )


def tendency(field, place, first, count, weights):
    def rows(c, dx, dz):
        return field[c, place + dx, pl.ds(first + dz, count), :]

    centers = [rows(c, 0, 0) for c in range(3)]
    lanes = centers[0].shape[1]
    along_x = centers[0] * (1.0 / (12.0 * STEP_X))
    along_z = centers[2] * (1.0 / (12.0 * STEP_Z))
    results = []
    for c in range(3):
        center = centers[c]
        x2, x1, x_1, x_2 = (rows(c, d, 0) for d in (2, 1, -1, -2))
        z2, z1, z_1, z_2 = (rows(c, 0, d) for d in (2, 1, -1, -2))
        upper = pltpu.roll(center, lanes - 1, 1)
        lower = pltpu.roll(center, 1, 1)
        slope_x = 8.0 * (x1 - x_1) - (x2 - x_2)
        slope_z = 8.0 * (z1 - z_1) - (z2 - z_2)
        slope_y = weights[0] * upper + weights[1] * lower + weights[2] * center
        curve_x = 16.0 * (x1 + x_1) - (x2 + x_2) - 30.0 * center
        curve_z = 16.0 * (z1 + z_1) - (z2 + z_2) - 30.0 * center
        curve_y = weights[3] * upper + weights[4] * center + weights[5] * lower
        carried = along_x * slope_x + centers[1] * slope_y + along_z * slope_z
        spread = (
            curve_x * (VISCOSITY / (12.0 * STEP_X * STEP_X))
            + curve_z * (VISCOSITY / (12.0 * STEP_Z * STEP_Z))
            + curve_y
        )
        results.append((center, spread - carried))
    return results


PACKED_ROWS = 80


def pack_gram(gram, packed_ref):
    half = gram.shape[0] // 2
    first, second = gram[:half], gram[half:]
    row = lax.broadcasted_iota(jnp.int32, first.shape, 0)
    lane = lax.broadcasted_iota(jnp.int32, first.shape, 1)
    packed_ref[0:half, :] = jnp.where(lane < row, pltpu.roll(second, half, 1), first)
    diagonal = jnp.sum(jnp.where(lane == row + half, second, 0.0), axis=0, keepdims=True)
    packed_ref[half:, :] = jnp.broadcast_to(diagonal, (PACKED_ROWS - half, gram.shape[1]))


def unpack_gram(packed_ref, gram_ref):
    size = gram_ref.shape[0]
    half = size // 2
    kept = packed_ref[0:half, :]
    turned = jnp.concatenate([kept, jnp.zeros_like(kept)], 0).T[0:half]
    row = lax.broadcasted_iota(jnp.int32, kept.shape, 0)
    lane = lax.broadcasted_iota(jnp.int32, kept.shape, 1)
    gram_ref[0:half, :] = jnp.where(lane < row, turned, kept)
    second = pltpu.roll(jnp.where(lane < row, kept, turned), half, 1)
    diagonal = jnp.broadcast_to(packed_ref[half : half + 1, :], kept.shape)
    gram_ref[half:, :] = jnp.where(lane == row + half, diagonal, second)


CHUNKS = (128, 128, 128)
MXU_STEP = 32


def step_kernel(
    scale,
    velocity_ref,
    left_ref,
    right_ref,
    behind_ref,
    ahead_ref,
    weights_ref,
    basis_ref,
    stored_ref,
    advanced_ref,
    packed_ref,
    block,
    wide,
    folded,
    field,
    section,
    advanced,
    sems,
    halo_sems,
    out_sem,
):
    n_basis = basis_ref.shape[0]
    n_stored = stored_ref.shape[0]
    length_x, length_z = velocity_ref.shape[1:3]
    starts = [sum(CHUNKS[:q]) for q in range(len(CHUNKS))]

    halos = [
        pltpu.make_async_copy(source, target, halo_sems.at[i])
        for i, (source, target) in enumerate(
            (
                (velocity_ref, field.at[:, pl.ds(4, length_x), pl.ds(4, length_z)]),
                (left_ref, field.at[:, pl.ds(0, 4), pl.ds(4, length_z)]),
                (right_ref, field.at[:, pl.ds(4 + length_x, 4), pl.ds(4, length_z)]),
                (behind_ref, field.at[:, pl.ds(2, 4 + length_x), pl.ds(0, 4)]),
                (ahead_ref, field.at[:, pl.ds(2, 4 + length_x), pl.ds(4 + length_z, 4)]),
            )
        )
    ]
    for halo in halos:
        halo.start()

    def send(q, source, column, place):
        span = pl.ds(starts[q], CHUNKS[q])
        pltpu.make_async_copy(
            source.at[column, span],
            block.at[span, pl.ds(pl.multiple_of(2 * (place + column), 2), 2)],
            sems.at[q],
        ).start()

    def issue_part(q, part, parts):
        for source, place in ((basis_ref, 0), (stored_ref, n_basis)):
            share = source.shape[0] // parts
            for i in range(share):
                send(q, source, part * share + i, place)

    def issue_rest(q, parts):
        for source, place in ((basis_ref, 0), (stored_ref, n_basis)):
            for column in range(source.shape[0] // parts * parts, source.shape[0]):
                send(q, source, column, place)

    def section_plane(x):
        for c, (center, change) in enumerate(tendency(field, x + 2, 2, length_z + 8, weights)):
            section[c, x, pl.ds(0, length_z + 8), :] = center + TIME_STEP * change

    @pl.loop(0, 8)
    def _(part):
        issue_part(0, part, 8)

    issue_rest(0, 8)
    for halo in halos:
        halo.wait()

    weights = [weights_ref[i : i + 1, :] for i in range(6)]

    @pl.loop(0, length_x)
    def _(x):
        issue_part(1, x, length_x)
        section_plane(x)

    issue_rest(1, length_x)

    @pl.loop(length_x, length_x + 4)
    def _(x):
        section_plane(x)

    last = 2 * (n_basis + n_stored)

    @pl.loop(0, length_x)
    def _(x):
        issue_part(2, x, length_x)
        for c, (center, change) in enumerate(tendency(section, x + 2, 2, length_z, weights)):
            begin = field[c, x + 4, pl.ds(4, length_z), :]
            end = 0.5 * (begin + center + TIME_STEP * change)
            advanced[c, x] = end
            rounded = end.astype(jnp.bfloat16)
            pair = (c * length_x + x) * (length_z // 2)
            for j in range(length_z // 2):
                block[pair + j, last : last + 2, :] = rounded[2 * j : 2 * j + 2, :]

    issue_rest(2, length_x)

    leave = pltpu.make_async_copy(advanced, advanced_ref, out_sem.at[0])
    leave.start()

    def body(acc0, acc1):
        accs = (acc0, acc1)
        for q in range(len(CHUNKS)):
            arrived = block.at[pl.ds(starts[q], CHUNKS[q]), pl.ds(0, last)]
            pltpu.make_async_copy(arrived, arrived, sems.at[q]).wait()

            @pl.loop(0, CHUNKS[q] // MXU_STEP)
            def _(t):
                base = starts[q] + t * MXU_STEP
                for u in range(MXU_STEP // 2):
                    unit = u % 2
                    register = (u // 2) % 2
                    rows = jnp.concatenate([block[base + 2 * u], block[base + 2 * u + 1]], axis=1)
                    pltpu.matmul_push_rhs(rows, register, unit, transpose=True)
                    pltpu.matmul_acc_lhs(accs[unit], rows, load_staged_rhs=register)

        total = pltpu.matmul_pop(acc0) + pltpu.matmul_pop(acc1)
        for h in range(2):
            wide[h] = total[:, 128 * h : 128 * (h + 1)]

    pl.run_scoped(
        body, pltpu.ACC(0)((256, 256), jnp.float32), pltpu.ACC(1)((256, 256), jnp.float32)
    )
    lane = lax.broadcasted_iota(jnp.int32, (128, 128), 1)
    for h in range(2):
        even = wide[h, pl.ds(0, 128, stride=2), :]
        odd = wide[h, pl.ds(1, 128, stride=2), :]
        folded[128 * h : 128 * (h + 1)] = (jnp.where(lane % 2 == 0, even, odd) * scale).T
    gram = folded[pl.ds(0, 128, stride=2), :] + folded[pl.ds(1, 128, stride=2), :]
    pack_gram(gram, packed_ref)
    leave.wait()


def pair_rows(fields):
    return fields.reshape(fields.shape[0], -1, 2, fields.shape[-1])


def step_and_gram(velocity, halos, weights, basis, stored, scale):
    basis = pltpu.with_memory_space_constraint(pair_rows(basis), pltpu.HBM)
    stored = pltpu.with_memory_space_constraint(pair_rows(stored), pltpu.HBM)
    velocity = pltpu.with_memory_space_constraint(velocity, pltpu.HBM)
    length_x, length_z, lanes = velocity.shape[1:]
    hbm = pl.BlockSpec(memory_space=pltpu.HBM)
    free = pl.BlockSpec(memory_space=pl.ANY)
    vmem = pl.BlockSpec(memory_space=pltpu.VMEM)
    return pl.pallas_call(
        functools.partial(step_kernel, scale),
        out_shape=(
            jax.ShapeDtypeStruct(velocity.shape, jnp.float32),
            jax.ShapeDtypeStruct((PACKED_ROWS, 128), jnp.float32),
        ),
        in_specs=[hbm, free, free, free, free, vmem, hbm, hbm],
        out_specs=(hbm, vmem),
        scratch_shapes=[
            pltpu.VMEM((basis.shape[1], 256, lanes), jnp.bfloat16),
            pltpu.VMEM((2, 256, 128), jnp.float32),
            pltpu.VMEM((256, 128), jnp.float32),
            pltpu.VMEM((3, length_x + 8, length_z + 16, lanes), jnp.float32),
            pltpu.VMEM((3, length_x + 4, length_z + 8, lanes), jnp.float32),
            pltpu.VMEM(velocity.shape, jnp.float32),
            pltpu.SemaphoreType.DMA((len(CHUNKS),)),
            pltpu.SemaphoreType.DMA((5,)),
            pltpu.SemaphoreType.DMA((1,)),
        ],
        compiler_params=pltpu.CompilerParams(vmem_limit_bytes=36 * 2**20),
        name="step_gram",
    )(velocity, *halos, weights, basis, stored)


def shift(part, axis, step):
    count = lax.axis_size(axis)
    return lax.ppermute(part, axis, [(i, (i + step) % count) for i in range(count)])


def exchange(velocity):
    left = shift(velocity[:, -4:], "gx", 1)
    right = shift(velocity[:, :4], "gx", -1)
    back, front = lax.optimization_barrier((velocity[:, :, -4:], velocity[:, :, :4]))
    back = jnp.concatenate([left[:, 2:, -4:], back, right[:, :2, -4:]], axis=1)
    front = jnp.concatenate([left[:, 2:, :4], front, right[:, :2, :4]], axis=1)
    count = lax.axis_size("gy")
    first = lax.axis_index("gy") % 2 == 0
    outer = lax.ppermute(
        jnp.where(first, front, back),
        "gy",
        [(i, (i + 2 * (i % 2) - 1) % count) for i in range(count)],
    )
    inner = swap_cores(jnp.where(first, back, front), count)
    behind = jnp.where(first, outer, inner)
    ahead = jnp.where(first, inner, outer)
    return left, right, behind, ahead


def wall_rows(points):
    up, down, here, curve_down, curve_here, curve_up = wall_weights(points)
    lane = jnp.arange(points)
    has_up = lane < points - 1
    has_down = lane > 0
    return jnp.stack(
        [
            jnp.where(has_up, up, 0.0),
            jnp.where(has_down, down, 0.0),
            here,
            VISCOSITY * jnp.where(has_up, curve_down, 0.0),
            VISCOSITY * curve_here,
            VISCOSITY * jnp.where(has_down, curve_up, 0.0),
            jnp.zeros_like(here),
            jnp.zeros_like(here),
        ]
    )


def swap_cores(part, count):
    return lax.ppermute(part, "gy", [(i, i ^ 1) for i in range(count)])


def group_sum(part, axis, members, groups=None):
    copies = jnp.broadcast_to(part[None], (members, *part.shape))
    return lax.all_to_all(copies, axis, 0, 0, axis_index_groups=groups).sum(0)


def ring_sum(part, axis):
    moved = [shift(part, axis, d) for d in (1, 2, 3)]
    return (part + moved[1]) + (moved[0] + moved[2])


def total_gram(packed):
    count = lax.axis_size("gy")
    half = packed.shape[0] // 2
    core = lax.axis_index("gy") % 2
    mine = lax.dynamic_slice_in_dim(packed, core * half, half, 0)
    other = lax.dynamic_slice_in_dim(packed, (1 - core) * half, half, 0)
    part = mine + swap_cores(other, count)
    part = group_sum(part, "gy", count // 2, [list(range(c, count, 2)) for c in range(2)])
    part = ring_sum(part, "gx")
    rest = swap_cores(part, count)
    low = jnp.where(core == 0, part, rest)
    high = jnp.where(core == 0, rest, part)
    return jnp.concatenate([low, high], 0)


PANEL = 16


def factor_kernel(packed_ref, factor_ref, work):
    size = work.shape[0]
    unpack_gram(packed_ref, work)
    row = lax.broadcasted_iota(jnp.int32, (PANEL, size), 0)
    lane = lax.broadcasted_iota(jnp.int32, (PANEL, size), 1)
    for begin in range(0, size, PANEL):
        end = begin + PANEL
        rows = work[begin:end, :]
        columns = [
            jnp.broadcast_to(rows[:, begin + k : begin + k + 1], (PANEL, size))
            for k in range(PANEL)
        ]
        scales = jnp.zeros((PANEL, size), jnp.float32)
        for j in range(PANEL):
            scale = lax.rsqrt(columns[j][j : j + 1, :])
            below = jnp.where(row > j, columns[j] * scale, 0.0)
            for k in range(j + 1, PANEL):
                columns[k] = columns[k] - below * (columns[k][j : j + 1, :] * scale)
            rows = rows - below * (rows[j : j + 1, :] * scale)
            scales = jnp.where(row == j, jnp.broadcast_to(scale, (PANEL, size)), scales)
        done = jnp.where(lane >= row + begin, rows * scales, 0.0)
        factor_ref[begin:end, :] = done
        if end < size:
            high = done.astype(jnp.bfloat16)
            left = done - high.astype(jnp.float32)
            mid = left.astype(jnp.bfloat16)
            low = (left - mid.astype(jnp.float32)).astype(jnp.bfloat16)
            product = lax.dot_general(
                jnp.concatenate([high, high, mid, high, low, mid], 0),
                jnp.concatenate([high, mid, high, low, high, mid], 0),
                (((0,), (0,)), ((), ())),
                preferred_element_type=jnp.float32,
            )
            work[end:, :] = work[end:, :] - product[end:, :]


def upper_factor(packed):
    shape = (packed.shape[1], packed.shape[1])
    return pl.pallas_call(
        factor_kernel,
        out_shape=jax.ShapeDtypeStruct(shape, jnp.float32),
        in_specs=[pl.BlockSpec(memory_space=pltpu.VMEM)],
        out_specs=pl.BlockSpec(memory_space=pltpu.VMEM),
        scratch_shapes=[pltpu.VMEM(shape, jnp.float32)],
        compiler_params=pltpu.CompilerParams(vmem_limit_bytes=8 * 2**20),
        name="upper_factor",
    )(packed)


def local(velocity, basis, snapshots):
    total_rows = (
        3.0
        * velocity.shape[1]
        * lax.axis_size("gx")
        * velocity.shape[2]
        * lax.axis_size("gy")
        * velocity.shape[3]
    )
    halos = exchange(velocity)
    weights = wall_rows(velocity.shape[3])
    advanced, packed = step_and_gram(velocity, halos, weights, basis, snapshots, 1.0 / total_rows)
    factor = upper_factor(total_gram(packed))
    return (advanced, factor)


def solution(mesh):
    return jax.shard_map(
        local,
        mesh=mesh,
        in_specs=(
            P(None, "gx", "gy", None),
            P(None, None, "gx", "gy", None),
            P(None, None, "gx", "gy", None),
        ),
        out_specs=(P(None, "gx", "gy", None), P()),
        check_vma=False,
    )
```

```python
import functools
import math

import jax
import jax.numpy as jnp
from jax import lax
from jax.experimental import pallas as pl
from jax.experimental.pallas import tpu as pltpu
from jax.sharding import PartitionSpec as P


TIME_STEP = 0.0002
VISCOSITY = 0.005
STEP_X = 0.0123
STEP_Z = 0.0092
STRETCH = 2.0


def wall_weights(points):
    positions = jnp.arange(points + 2, dtype=jnp.float32)
    nodes = -jnp.tanh(STRETCH * (1.0 - 2.0 * positions / (points + 1))) / math.tanh(STRETCH)
    below = nodes[1:-1] - nodes[:-2]
    above = nodes[2:] - nodes[1:-1]
    spread = above * below * (above + below)
    return (
        below * below / spread,
        -(above * above) / spread,
        (above * above - below * below) / spread,
        2.0 * below / spread,
        -2.0 * (above + below) / spread,
        2.0 * above / spread,
    )


def tendency(field, place, first, count, weights):
    def rows(c, dx, dz):
        return field[c, place + dx, pl.ds(first + dz, count), :]

    centers = [rows(c, 0, 0) for c in range(3)]
    lanes = centers[0].shape[1]
    along_x = centers[0] * (1.0 / (12.0 * STEP_X))
    along_z = centers[2] * (1.0 / (12.0 * STEP_Z))
    results = []
    for c in range(3):
        center = centers[c]
        x2, x1, x_1, x_2 = (rows(c, d, 0) for d in (2, 1, -1, -2))
        z2, z1, z_1, z_2 = (rows(c, 0, d) for d in (2, 1, -1, -2))
        upper = pltpu.roll(center, lanes - 1, 1)
        lower = pltpu.roll(center, 1, 1)
        slope_x = 8.0 * (x1 - x_1) - (x2 - x_2)
        slope_z = 8.0 * (z1 - z_1) - (z2 - z_2)
        slope_y = weights[0] * upper + weights[1] * lower + weights[2] * center
        curve_x = 16.0 * (x1 + x_1) - (x2 + x_2) - 30.0 * center
        curve_z = 16.0 * (z1 + z_1) - (z2 + z_2) - 30.0 * center
        curve_y = weights[3] * upper + weights[4] * center + weights[5] * lower
        carried = along_x * slope_x + centers[1] * slope_y + along_z * slope_z
        spread = (
            curve_x * (VISCOSITY / (12.0 * STEP_X * STEP_X))
            + curve_z * (VISCOSITY / (12.0 * STEP_Z * STEP_Z))
            + curve_y
        )
        results.append((center, spread - carried))
    return results


PACKED_ROWS = 80


def pack_gram(gram, packed_ref):
    half = gram.shape[0] // 2
    first, second = gram[:half], gram[half:]
    row = lax.broadcasted_iota(jnp.int32, first.shape, 0)
    lane = lax.broadcasted_iota(jnp.int32, first.shape, 1)
    packed_ref[0:half, :] = jnp.where(lane < row, pltpu.roll(second, half, 1), first)
    diagonal = jnp.sum(jnp.where(lane == row + half, second, 0.0), axis=0, keepdims=True)
    packed_ref[half:, :] = jnp.broadcast_to(diagonal, (PACKED_ROWS - half, gram.shape[1]))


def unpack_gram(packed_ref, gram_ref):
    size = gram_ref.shape[0]
    half = size // 2
    kept = packed_ref[0:half, :]
    turned = jnp.concatenate([kept, jnp.zeros_like(kept)], 0).T[0:half]
    row = lax.broadcasted_iota(jnp.int32, kept.shape, 0)
    lane = lax.broadcasted_iota(jnp.int32, kept.shape, 1)
    gram_ref[0:half, :] = jnp.where(lane < row, turned, kept)
    second = pltpu.roll(jnp.where(lane < row, kept, turned), half, 1)
    diagonal = jnp.broadcast_to(packed_ref[half : half + 1, :], kept.shape)
    gram_ref[half:, :] = jnp.where(lane == row + half, diagonal, second)


CHUNKS = (128, 128, 128)
MXU_STEP = 64


def step_kernel(
    scale,
    velocity_ref,
    left_ref,
    right_ref,
    far_left_ref,
    far_right_ref,
    behind_ref,
    ahead_ref,
    weights_ref,
    basis_ref,
    stored_ref,
    advanced_ref,
    packed_ref,
    block,
    wide,
    folded,
    field,
    section,
    advanced,
    sems,
    halo_sems,
    out_sem,
):
    n_basis = basis_ref.shape[0]
    n_stored = stored_ref.shape[0]
    length_x, length_z = velocity_ref.shape[1:3]
    starts = [sum(CHUNKS[:q]) for q in range(len(CHUNKS))]

    halos = [
        pltpu.make_async_copy(source, target, halo_sems.at[i])
        for i, (source, target) in enumerate(
            (
                (velocity_ref, field.at[:, pl.ds(4, length_x), pl.ds(4, length_z)]),
                (left_ref, field.at[:, pl.ds(2, 2), pl.ds(4, length_z)]),
                (right_ref, field.at[:, pl.ds(4 + length_x, 2), pl.ds(4, length_z)]),
                (far_left_ref, field.at[:, pl.ds(0, 2), pl.ds(4, length_z)]),
                (far_right_ref, field.at[:, pl.ds(6 + length_x, 2), pl.ds(4, length_z)]),
                (behind_ref, field.at[:, pl.ds(2, 4 + length_x), pl.ds(0, 4)]),
                (ahead_ref, field.at[:, pl.ds(2, 4 + length_x), pl.ds(4 + length_z, 4)]),
            )
        )
    ]
    for halo in halos:
        halo.start()

    def send(q, source, column, place):
        span = pl.ds(starts[q], CHUNKS[q])
        pltpu.make_async_copy(
            source.at[column, span],
            block.at[span, pl.ds(pl.multiple_of(2 * (place + column), 2), 2)],
            sems.at[q],
        ).start()

    def issue_part(q, part, parts):
        for source, place in ((basis_ref, 0), (stored_ref, n_basis)):
            share = source.shape[0] // parts
            for i in range(share):
                send(q, source, part * share + i, place)

    def issue_rest(q, parts):
        for source, place in ((basis_ref, 0), (stored_ref, n_basis)):
            for column in range(source.shape[0] // parts * parts, source.shape[0]):
                send(q, source, column, place)

    def section_plane(x):
        for c, (center, change) in enumerate(tendency(field, x + 2, 2, length_z + 8, weights)):
            section[c, x, pl.ds(0, length_z + 8), :] = center + TIME_STEP * change

    @pl.loop(0, 8)
    def _(part):
        issue_part(0, part, 8)

    issue_rest(0, 8)
    for halo in halos:
        halo.wait()

    weights = [weights_ref[i : i + 1, :] for i in range(6)]

    @pl.loop(0, length_x)
    def _(x):
        issue_part(1, x, length_x)
        section_plane(x)

    issue_rest(1, length_x)

    @pl.loop(length_x, length_x + 4)
    def _(x):
        section_plane(x)

    last = 2 * (n_basis + n_stored)

    @pl.loop(0, length_x)
    def _(x):
        issue_part(2, x, length_x)
        for c, (center, change) in enumerate(tendency(section, x + 2, 2, length_z, weights)):
            begin = field[c, x + 4, pl.ds(4, length_z), :]
            end = 0.5 * (begin + center + TIME_STEP * change)
            advanced[c, x] = end
            rounded = end.astype(jnp.bfloat16)
            pair = (c * length_x + x) * (length_z // 2)
            for j in range(length_z // 2):
                block[pair + j, last : last + 2, :] = rounded[2 * j : 2 * j + 2, :]

    issue_rest(2, length_x)

    leave = pltpu.make_async_copy(advanced, advanced_ref, out_sem.at[0])
    leave.start()

    def body(acc0, acc1):
        accs = (acc0, acc1)
        for q in range(len(CHUNKS)):
            arrived = block.at[pl.ds(starts[q], CHUNKS[q]), pl.ds(0, last)]
            pltpu.make_async_copy(arrived, arrived, sems.at[q]).wait()

            @pl.loop(0, CHUNKS[q] // MXU_STEP)
            def _(t):
                base = starts[q] + t * MXU_STEP
                for u in range(MXU_STEP // 2):
                    unit = u % 2
                    register = (u // 2) % 2
                    rows = jnp.concatenate([block[base + 2 * u], block[base + 2 * u + 1]], axis=1)
                    pltpu.matmul_push_rhs(rows, register, unit, transpose=True)
                    pltpu.matmul_acc_lhs(accs[unit], rows, load_staged_rhs=register)

        total = pltpu.matmul_pop(acc0) + pltpu.matmul_pop(acc1)
        for h in range(2):
            wide[h] = total[:, 128 * h : 128 * (h + 1)]

    pl.run_scoped(
        body, pltpu.ACC(0)((256, 256), jnp.float32), pltpu.ACC(1)((256, 256), jnp.float32)
    )
    lane = lax.broadcasted_iota(jnp.int32, (128, 128), 1)
    for h in range(2):
        even = wide[h, pl.ds(0, 128, stride=2), :]
        odd = wide[h, pl.ds(1, 128, stride=2), :]
        folded[128 * h : 128 * (h + 1)] = (jnp.where(lane % 2 == 0, even, odd) * scale).T
    gram = folded[pl.ds(0, 128, stride=2), :] + folded[pl.ds(1, 128, stride=2), :]
    pack_gram(gram, packed_ref)
    leave.wait()


def pair_rows(fields):
    return fields.reshape(fields.shape[0], -1, 2, fields.shape[-1])


def step_and_gram(velocity, halos, weights, basis, stored, scale):
    basis = pltpu.with_memory_space_constraint(pair_rows(basis), pltpu.HBM)
    stored = pltpu.with_memory_space_constraint(pair_rows(stored), pltpu.HBM)
    velocity = pltpu.with_memory_space_constraint(velocity, pltpu.HBM)
    length_x, length_z, lanes = velocity.shape[1:]
    hbm = pl.BlockSpec(memory_space=pltpu.HBM)
    free = pl.BlockSpec(memory_space=pl.ANY)
    vmem = pl.BlockSpec(memory_space=pltpu.VMEM)
    return pl.pallas_call(
        functools.partial(step_kernel, scale),
        out_shape=(
            jax.ShapeDtypeStruct(velocity.shape, jnp.float32),
            jax.ShapeDtypeStruct((PACKED_ROWS, 128), jnp.float32),
        ),
        in_specs=[hbm, free, free, free, free, free, free, vmem, hbm, hbm],
        out_specs=(hbm, vmem),
        scratch_shapes=[
            pltpu.VMEM((basis.shape[1], 256, lanes), jnp.bfloat16),
            pltpu.VMEM((2, 256, 128), jnp.float32),
            pltpu.VMEM((256, 128), jnp.float32),
            pltpu.VMEM((3, length_x + 8, length_z + 16, lanes), jnp.float32),
            pltpu.VMEM((3, length_x + 4, length_z + 8, lanes), jnp.float32),
            pltpu.VMEM(velocity.shape, jnp.float32),
            pltpu.SemaphoreType.DMA((len(CHUNKS),)),
            pltpu.SemaphoreType.DMA((7,)),
            pltpu.SemaphoreType.DMA((1,)),
        ],
        compiler_params=pltpu.CompilerParams(vmem_limit_bytes=36 * 2**20),
        name="step_gram",
    )(velocity, *halos, weights, basis, stored)


def shift(part, axis, step):
    count = lax.axis_size(axis)
    return lax.ppermute(part, axis, [(i, (i + step) % count) for i in range(count)])


def exchange(velocity):
    left = shift(velocity[:, -2:], "gx", 1)
    right = shift(velocity[:, :2], "gx", -1)
    far_left = shift(velocity[:, -4:-2], "gx", 1)
    far_right = shift(velocity[:, 2:4], "gx", -1)
    back, front = lax.optimization_barrier((velocity[:, :, -4:], velocity[:, :, :4]))
    back = jnp.concatenate([left[:, :, -4:], back, right[:, :, -4:]], axis=1)
    front = jnp.concatenate([left[:, :, :4], front, right[:, :, :4]], axis=1)
    count = lax.axis_size("gy")
    first = lax.axis_index("gy") % 2 == 0
    outer = lax.ppermute(
        jnp.where(first, front, back),
        "gy",
        [(i, (i + 2 * (i % 2) - 1) % count) for i in range(count)],
    )
    inner = swap_cores(jnp.where(first, back, front), count)
    behind = jnp.where(first, outer, inner)
    ahead = jnp.where(first, inner, outer)
    return left, right, far_left, far_right, behind, ahead


def wall_rows(points):
    up, down, here, curve_down, curve_here, curve_up = wall_weights(points)
    lane = jnp.arange(points)
    has_up = lane < points - 1
    has_down = lane > 0
    return jnp.stack(
        [
            jnp.where(has_up, up, 0.0),
            jnp.where(has_down, down, 0.0),
            here,
            VISCOSITY * jnp.where(has_up, curve_down, 0.0),
            VISCOSITY * curve_here,
            VISCOSITY * jnp.where(has_down, curve_up, 0.0),
            jnp.zeros_like(here),
            jnp.zeros_like(here),
        ]
    )


def swap_cores(part, count):
    return lax.ppermute(part, "gy", [(i, i ^ 1) for i in range(count)])


def group_sum(part, axis, members, groups=None):
    copies = jnp.broadcast_to(part[None], (members, *part.shape))
    return lax.all_to_all(copies, axis, 0, 0, axis_index_groups=groups).sum(0)


def ring_sum(part, axis):
    moved = [shift(part, axis, d) for d in (1, 2, 3)]
    return (part + moved[1]) + (moved[0] + moved[2])


def total_gram(packed):
    count = lax.axis_size("gy")
    half = packed.shape[0] // 2
    core = lax.axis_index("gy") % 2
    mine = lax.dynamic_slice_in_dim(packed, core * half, half, 0)
    other = lax.dynamic_slice_in_dim(packed, (1 - core) * half, half, 0)
    part = mine + swap_cores(other, count)
    part = group_sum(part, "gy", count // 2, [list(range(c, count, 2)) for c in range(2)])
    part = ring_sum(part, "gx")
    rest = swap_cores(part, count)
    low = jnp.where(core == 0, part, rest)
    high = jnp.where(core == 0, rest, part)
    return jnp.concatenate([low, high], 0)


PANEL = 16


def factor_kernel(packed_ref, factor_ref, work):
    size = work.shape[0]
    unpack_gram(packed_ref, work)
    row = lax.broadcasted_iota(jnp.int32, (PANEL, size), 0)
    lane = lax.broadcasted_iota(jnp.int32, (PANEL, size), 1)
    for begin in range(0, size, PANEL):
        end = begin + PANEL
        rows = work[begin:end, :]
        columns = [
            jnp.broadcast_to(rows[:, begin + k : begin + k + 1], (PANEL, size))
            for k in range(PANEL)
        ]
        scales = jnp.zeros((PANEL, size), jnp.float32)
        for j in range(PANEL):
            scale = lax.rsqrt(columns[j][j : j + 1, :])
            below = jnp.where(row > j, columns[j] * scale, 0.0)
            for k in range(j + 1, PANEL):
                columns[k] = columns[k] - below * (columns[k][j : j + 1, :] * scale)
            rows = rows - below * (rows[j : j + 1, :] * scale)
            scales = jnp.where(row == j, jnp.broadcast_to(scale, (PANEL, size)), scales)
        done = jnp.where(lane >= row + begin, rows * scales, 0.0)
        factor_ref[begin:end, :] = done
        if end < size:
            high = done.astype(jnp.bfloat16)
            left = done - high.astype(jnp.float32)
            mid = left.astype(jnp.bfloat16)
            low = (left - mid.astype(jnp.float32)).astype(jnp.bfloat16)
            product = lax.dot_general(
                jnp.concatenate([high, high, mid, high, low, mid], 0),
                jnp.concatenate([high, mid, high, low, high, mid], 0),
                (((0,), (0,)), ((), ())),
                preferred_element_type=jnp.float32,
            )
            work[end:, :] = work[end:, :] - product[end:, :]


def upper_factor(packed):
    shape = (packed.shape[1], packed.shape[1])
    return pl.pallas_call(
        factor_kernel,
        out_shape=jax.ShapeDtypeStruct(shape, jnp.float32),
        in_specs=[pl.BlockSpec(memory_space=pltpu.VMEM)],
        out_specs=pl.BlockSpec(memory_space=pltpu.VMEM),
        scratch_shapes=[pltpu.VMEM(shape, jnp.float32)],
        compiler_params=pltpu.CompilerParams(vmem_limit_bytes=8 * 2**20),
        name="upper_factor",
    )(packed)


def local(velocity, basis, snapshots):
    total_rows = (
        3.0
        * velocity.shape[1]
        * lax.axis_size("gx")
        * velocity.shape[2]
        * lax.axis_size("gy")
        * velocity.shape[3]
    )
    halos = exchange(velocity)
    weights = wall_rows(velocity.shape[3])
    advanced, packed = step_and_gram(velocity, halos, weights, basis, snapshots, 1.0 / total_rows)
    factor = upper_factor(total_gram(packed))
    return (advanced, factor)


def solution(mesh):
    return jax.shard_map(
        local,
        mesh=mesh,
        in_specs=(
            P(None, "gx", "gy", None),
            P(None, None, "gx", "gy", None),
            P(None, None, "gx", "gy", None),
        ),
        out_specs=(P(None, "gx", "gy", None), P()),
        check_vma=False,
    )
```
